256 devices in a mesh: tm: 32 (over x, z), space: 8 (over y, core).
Axes of the slice: x: 4, y: 4, z: 8, core: 2. Of those that a mesh axis runs over, the one named last changes fastest.
Arguments:
- density: float32 [128, 512, 512], P('tm', 'space'), may hold values from 0.2 to 2
- flux_x: float32 [128, 512, 512], P('tm', 'space'), may hold values from -5 to 5
- flux_y: float32 [128, 512, 512], P('tm', 'space'), may hold values from -5 to 5
- source: float32 [128, 512, 512], P('tm', 'space'), may hold values from -0.3 to 0.3
Outputs:
- new_density: float32 [128, 512, 512], P('tm', 'space')
- new_flux_x: float32 [128, 512, 512], P('tm', 'space')
- new_flux_y: float32 [128, 512, 512], P('tm', 'space')
- potential: float32 [128, 512, 512], P('tm', 'space')
The draws below stay inside these ranges and needn't reach their ends.
All inputs are finite; a program needn't handle non-finite values.
Results may differ from the reference program's by a relative error of at most 0.0003.
Values sent between devices are 32-bit elements; how exact they have to be, the bound alone decides.
No kernel may reach another device: no remote copies, remote signals or barrier semaphores. Data moves between devices by JAX's collectives and lax.ppermute only.
A program may use at most 128 MiB of HBM per device.

```python
import jax
import jax.numpy as jnp
from jax import lax

NS = 512
ITERS = 3
NEWTON = 10
TIME = 128


def shard_levels(key, dims, split, least, top_value):
    def one(dim, shards_of):
        heights = jax.random.uniform(jax.random.fold_in(jax.random.fold_in(key, 6), dim), (shards_of,), jnp.float32, least / len(split), top_value / len(split))
        return jnp.repeat(jnp.exp(heights), dims[dim] // shards_of).reshape((-1,) + (1,) * (len(dims) - dim - 1))

    level = one(*split[0])
    for cut in split[1:]:
        level = level * one(*cut)
    return level


def scatter_about(rng, shape, scale, reach, shards=(), kind=jnp.bfloat16):
    array = scale * jax.random.normal(rng, shape, jnp.float32)
    if shards:
        array = array * shard_levels(rng, shape, shards, -0.22, 0.18)
    return jnp.clip(array, -reach, reach).astype(kind)


def setup_inputs(seed: int = 0) -> dict:
    streams_of = jax.random.split(jax.random.key(seed), 5)
    return {
        "density": jnp.clip(0.2 + 1.8 * jax.random.uniform(streams_of[0], (TIME, NS, NS), jnp.float32) ** shard_levels(streams_of[0], (TIME, NS, NS), ((0, 32), (1, 8)), -0.2, 0.2), 0.2, 2.0),
        "flux_x": scatter_about(streams_of[1], (TIME, NS, NS), 1.0, 5.0, ((0, 32), (1, 8)), jnp.float32),
        "flux_y": scatter_about(streams_of[2], (TIME, NS, NS), 1.0, 5.0, ((0, 32), (1, 8)), jnp.float32),
        "source": scatter_about(streams_of[3], (TIME, NS, NS), 0.05, 0.3, ((0, 32), (1, 8)), jnp.float32),
    }


TAU_STEP = 1.0
SLOW_LOOP = 2.25

def cosine_matrix(points):
    frequency = jnp.arange(points, dtype=jnp.float32)[:, None]
    sample = jnp.arange(points, dtype=jnp.float32)[None, :]
    scaling = jnp.where(frequency == 0, jnp.sqrt(1.0 / points), jnp.sqrt(2.0 / points))
    return (scaling * jnp.cos(jnp.pi * (sample + 0.5) * frequency / points)).astype(jnp.float32)

def neumann_spectrum(points):
    half_angle = jnp.pi * jnp.arange(points, dtype=jnp.float32) / (2.0 * points)
    sine = jnp.sin(half_angle)
    return 4.0 * sine * sine

def flux_divergence(values, along_axis):
    swapped = jnp.moveaxis(values, along_axis, -1)
    points = swapped.shape[-1]
    inside = jnp.where(jnp.arange(points) < points - 1, swapped, 0.0)
    before = jnp.concatenate([jnp.zeros_like(swapped[..., :1]), swapped[..., :-1]], axis=-1)
    return jnp.moveaxis(inside - before, -1, along_axis)

def minus_gradient(values, along_axis):
    swapped = jnp.moveaxis(values, along_axis, -1)
    following = jnp.concatenate([swapped[..., 1:], swapped[..., -1:]], axis=-1)
    return jnp.moveaxis(swapped - following, -1, along_axis)

def kinetic_prox(mass_in, along_x, along_y):
    target = 0.5 * TAU_STEP * (along_x * along_x + along_y * along_y)
    newton_root = jnp.maximum(mass_in, 0.0) + jnp.cbrt(target)
    for newton_step in range(NEWTON):
        shifted = newton_root + TAU_STEP
        residue = (newton_root - mass_in) * shifted * shifted - target
        derivative = shifted * shifted + 2.0 * (newton_root - mass_in) * shifted
        newton_root = jnp.maximum(newton_root - residue / derivative, 0.0)
    factor = newton_root / (newton_root + TAU_STEP)
    return (newton_root, factor * along_x, factor * along_y)

def reference(density, flux_x, flux_y, source):
    highest = lax.Precision.HIGHEST
    screen = SLOW_LOOP / float(TIME * TIME)
    cosine = cosine_matrix(NS)
    spectrum = neumann_spectrum(NS)
    frequency = jnp.arange(TIME // 2 + 1, dtype=jnp.float32)
    time_sine = jnp.sin(jnp.pi * frequency / TIME)
    time_spectrum = 4.0 * time_sine * time_sine
    denominator = time_spectrum[:, None, None] + spectrum[None, :, None] + spectrum[None, None, :] + screen
    potential = jnp.zeros_like(density)
    adjoint_t = jnp.zeros_like(density)
    adjoint_x = jnp.zeros_like(density)
    adjoint_y = jnp.zeros_like(density)
    for iteration in range(ITERS):
        next_mass, next_x, next_y = kinetic_prox(density - TAU_STEP * adjoint_t, flux_x - TAU_STEP * adjoint_x, flux_y - TAU_STEP * adjoint_y)
        bar_mass = 2.0 * next_mass - density
        bar_x = 2.0 * next_x - flux_x
        bar_y = 2.0 * next_y - flux_y
        residual = bar_mass - jnp.roll(bar_mass, 1, axis=0) + flux_divergence(bar_x, 1) + flux_divergence(bar_y, 2) - source
        half_hat = jnp.einsum('tij,bj->tib', residual, cosine, precision=highest)
        spectral = jnp.einsum('tib,ai->tab', half_hat, cosine, precision=highest)
        solved = jnp.fft.irfft(jnp.fft.rfft(spectral, axis=0) / denominator, n=TIME, axis=0).astype(jnp.float32)
        half_back = jnp.einsum('tab,ai->tib', solved, cosine, precision=highest)
        update = jnp.einsum('tib,bj->tij', half_back, cosine, precision=highest)
        potential = potential + update
        adjoint_t = adjoint_t + update - jnp.roll(update, -1, axis=0)
        adjoint_x = adjoint_x + minus_gradient(update, 1)
        adjoint_y = adjoint_y + minus_gradient(update, 2)
        density, flux_x, flux_y = (next_mass, next_x, next_y)
    return (density, flux_x, flux_y, potential)
```

```python
import functools

import jax
import jax.numpy as jnp
import numpy as np
from jax import lax
from jax.experimental import pallas as pl
from jax.experimental.pallas import tpu as pltpu
from jax.sharding import PartitionSpec as P

ITERS = 3
NEWTON = 10
TAU_STEP = 1.0
SLOW_LOOP = 2.25
INTERPRET = False
BOTH = ("tm", "space")
f32 = jnp.float32
bf16 = jnp.bfloat16
NN = (((1,), (0,)), ((), ()))
NT = (((1,), (1,)), ((), ()))
TN = (((0,), (0,)), ((), ()))


def halves(value):
    high = value.astype(bf16)
    return high, (value - high.astype(f32)).astype(bf16)


def dot3(left, right, dims):
    dot = functools.partial(lax.dot_general, dimension_numbers=dims, preferred_element_type=f32)
    return dot(left[0], right[0]) + (dot(left[0], right[1]) + dot(left[1], right[0]))


def cosine_matrix(points):
    one = np.float32
    frequency = np.arange(points, dtype=one)[:, None]
    sample = np.arange(points, dtype=one)[None, :]
    scaling = np.where(frequency == 0, np.sqrt(one(1.0 / points)), np.sqrt(one(2.0 / points))).astype(one)
    angle = one(np.pi) * (sample + one(0.5)) * frequency / one(points)
    return (scaling * np.cos(angle.astype(np.float64)).astype(one)).astype(one)


def neumann_spectrum(points):
    half_angle = np.pi * np.arange(points) / (2.0 * points)
    return (4.0 * np.sin(half_angle) ** 2).astype(np.float32)


def loop_basis(length, slabs):
    rows = [np.full(length, np.sqrt(1.0 / length))]
    values = [0.0]
    moment = np.arange(length)
    for k in range(1, length // 2):
        angle = 2.0 * np.pi * ((k * moment) % length) / length
        rows += [np.sqrt(2.0 / length) * np.cos(angle), np.sqrt(2.0 / length) * np.sin(angle)]
        values += [4.0 * np.sin(np.pi * k / length) ** 2] * 2
    rows.append(np.sqrt(1.0 / length) * (-1.0) ** moment)
    values.append(4.0)
    basis = np.stack(rows).reshape(length, slabs, length // slabs).transpose(0, 2, 1).reshape(length, length)
    return basis.astype(np.float32), np.asarray(values, np.float32)


def np_halves(matrix):
    high = matrix.astype(bf16)
    return high, (matrix - high.astype(np.float32)).astype(bf16)


def call(body, outs, scratch=(), scalars=0, n_in=0, cost=None, **kw):
    vmem = pl.BlockSpec(memory_space=pltpu.VMEM)
    smem = pl.BlockSpec(memory_space=pltpu.SMEM)
    return pl.pallas_call(
        body,
        out_shape=[jax.ShapeDtypeStruct(s, f32) for s in outs],
        in_specs=[smem] * scalars + [vmem] * n_in,
        out_specs=[vmem] * len(outs),
        scratch_shapes=list(scratch),
        cost_estimate=pl.CostEstimate(flops=int(cost[0]), bytes_accessed=int(cost[1]), transcendentals=0),
        interpret=INTERPRET,
        **kw,
    )


def newton(mass, along_x, along_y):
    target = 0.5 * TAU_STEP * (along_x * along_x + along_y * along_y)
    root = jnp.maximum(mass, 0.0) + jnp.exp(jnp.log(target) * (1.0 / 3.0))
    for _ in range(NEWTON):
        shifted = root + TAU_STEP
        gap = root - mass
        product = gap * shifted
        residue = product * shifted - target
        derivative = shifted * (shifted + (gap + gap))
        root = jnp.maximum(root - residue / derivative, 0.0)
    factor = root / (root + TAU_STEP)
    return root, factor * along_x, factor * along_y


def last_of(shape, axis, count):
    return lax.broadcasted_iota(jnp.int32, shape, axis) == count - 1


def prox_body(with_dual, last_place, *refs):
    if with_dual:
        place, d, fx, fy, u, u_plane, u_rows, nd, nx, ny, bar_plane, bar_rows = refs
    else:
        place, d, fx, fy, nd, nx, ny, bar_plane, bar_rows = refs
        u = None
    steps, rows, width = d.shape
    chunk = 16
    per = rows // chunk
    if with_dual:
        end_row = last_of((rows, width), 0, rows)
        end_column = last_of((rows, width), 1, width)
        for t in range(steps):
            here = u[t]
            later = u[t + 1] if t + 1 < steps else u_plane[...]
            edge = jnp.where(place[0] == last_place, here[rows - 1 :, :], u_rows[t : t + 1, :])
            below = jnp.where(end_row, edge, pltpu.roll(here, rows - 1, 0))
            right = jnp.where(end_column, here, pltpu.roll(here, width - 1, 1))
            nd[t] = d[t] - TAU_STEP * (here - later)
            nx[t] = fx[t] - TAU_STEP * (here - below)
            ny[t] = fy[t] - TAU_STEP * (here - right)
    source = (nd, nx, ny) if with_dual else (d, fx, fy)

    def step(index, carry):
        t = index // per
        span = pl.ds(pl.multiple_of((index % per) * chunk, chunk), chunk)
        out = newton(*[ref[t, span, :] for ref in source])
        for ref, value in zip((nd, nx, ny), out):
            ref[t, span, :] = value
        return carry

    lax.fori_loop(0, steps * per, step, 0)
    bar_plane[...] = 2.0 * nd[steps - 1] - d[steps - 1]
    for t in range(steps):
        bar_rows[t : t + 1, :] = 2.0 * nx[t, rows - 1 :, :] - fx[t, rows - 1 :, :]


def forward_body(last_place, place, d, fx, fy, nd, nx, ny, src, bar_plane, bar_rows, ch, cl, out, rh, rl):
    steps, rows, width = d.shape
    shape = (rows, width)
    row = lax.broadcasted_iota(jnp.int32, shape, 0)
    column = lax.broadcasted_iota(jnp.int32, shape, 1)
    final_row = (row == rows - 1) & (place[0] == last_place)
    before = bar_plane[...]
    for t in range(steps):
        mass = 2.0 * nd[t] - d[t]
        along_x = 2.0 * nx[t] - fx[t]
        along_y = 2.0 * ny[t] - fy[t]
        x_before = jnp.where(row == 0, bar_rows[t : t + 1, :], pltpu.roll(along_x, 1, 0))
        y_before = jnp.where(column == 0, 0.0, pltpu.roll(along_y, 1, 1))
        value = mass - before
        value = value + (jnp.where(final_row, 0.0, along_x) - x_before)
        value = value + (jnp.where(column == width - 1, 0.0, along_y) - y_before)
        value = value - src[t]
        before = mass
        high, low = halves(value)
        rh[t * rows : (t + 1) * rows, :] = high
        rl[t * rows : (t + 1) * rows, :] = low
    modes = dot3((ch[...], cl[...]), (rh[...], rl[...]), NT)
    lanes = 2 * rows
    for pair in range(steps // 2):
        out[pl.ds(pair, width, stride=steps // 2), :] = modes[:, pair * lanes : (pair + 1) * lanes]


def solve_body(slabs, places, steps, with_sum, *refs):
    if with_sum:
        z, ch, cl, wh, wl, vh, vl, den, so_far, out, total, field = refs
    else:
        z, ch, cl, wh, wl, vh, vl, den, out, total, field = refs
    length = slabs * steps
    pairs = steps // 2
    stride = places * 2 * pairs
    lanes = z.shape[1]
    low_half = lax.broadcasted_iota(jnp.int32, (slabs, lanes), 1) < lanes // 2

    def at(place, mode, pair):
        return pl.ds((place * 2 + mode) * pairs + pair, slabs, stride=stride)

    for mode in range(2):
        for pair in range(pairs):
            for q in range(places // 2):
                a = z[at(2 * q, mode, pair), :]
                b = z[at(2 * q + 1, mode, pair), :]
                top = mode * length + 2 * pair * slabs
                span = slice(q * lanes, (q + 1) * lanes)
                field[top : top + slabs, span] = jnp.where(low_half, a, pltpu.roll(b, lanes // 2, 1))
                field[top + slabs : top + 2 * slabs, span] = jnp.where(low_half, pltpu.roll(a, lanes // 2, 1), b)
    cosine = (ch[...], cl[...])
    for mode in range(2):
        span = slice(mode * length, (mode + 1) * length)
        field[span, :] = dot3((wh[...], wl[...]), halves(field[span, :]), NN)
    solved = dot3(halves(field[...]), cosine, NT) / den[...]
    if with_sum:
        solved = solved + so_far[...]
    total[...] = solved
    field[...] = dot3(halves(solved), cosine, NN)
    for mode in range(2):
        span = slice(mode * length, (mode + 1) * length)
        field[span, :] = dot3((vh[...], vl[...]), halves(field[span, :]), NN)
    for mode in range(2):
        for pair in range(pairs):
            for q in range(places // 2):
                top = mode * length + 2 * pair * slabs
                span = slice(q * lanes, (q + 1) * lanes)
                a = field[top : top + slabs, span]
                b = field[top + slabs : top + 2 * slabs, span]
                out[at(2 * q, mode, pair), :] = jnp.where(low_half, a, pltpu.roll(b, lanes // 2, 1))
                out[at(2 * q + 1, mode, pair), :] = jnp.where(low_half, pltpu.roll(a, lanes // 2, 1), b)


def backward_body(y, ch, cl, u, u_plane, u_rows):
    steps, rows, width = u.shape
    pairs = steps // 2
    cosine = (ch[...], cl[...])
    for pair in range(pairs):
        modes = halves(y[pl.ds(pair, width, stride=pairs), :])
        value = dot3(modes, cosine, TN)
        for half in range(2):
            t = 2 * pair + half
            u[t] = value[half * rows : (half + 1) * rows, :]
            u_rows[t : t + 1, :] = value[half * rows : half * rows + 1, :]
    u_plane[...] = u[0]


def local(density, flux_x, flux_y, source):
    steps, rows, width = density.shape
    slabs = lax.axis_size("tm")
    places = lax.axis_size("space")
    length = steps * slabs
    screen = SLOW_LOOP / float(length * length)
    ch, cl = (jnp.asarray(m) for m in np_halves(cosine_matrix(width)))
    basis, loop_values = loop_basis(length, slabs)
    wh, wl = (jnp.asarray(m) for m in np_halves(basis))
    vh, vl = (jnp.asarray(m) for m in np_halves(np.ascontiguousarray(basis.T)))
    spectrum = jnp.asarray(neumann_spectrum(width))
    place = lax.axis_index("space")
    first = 2 * (lax.axis_index("tm") * places + place)
    own = lax.dynamic_slice_in_dim(spectrum, first, 2)
    den = own[:, None, None] + jnp.asarray(loop_values)[None, :, None] + spectrum[None, None, :] + screen
    den = den.reshape(2 * length, width)
    place = place.astype(jnp.int32).reshape(1)
    nbytes = density.size * 4
    mega = density.size * width * 6
    field = (steps, rows, width)
    edges = [(rows, width), (steps, width)]
    packed = (width * steps // 2, 2 * rows)
    chunk = packed[0] * packed[1] // (slabs * places)
    loop_next = [(i, (i + 1) % slabs) for i in range(slabs)]
    loop_back = [((i + 1) % slabs, i) for i in range(slabs)]
    row_next = [(i, i + 1) for i in range(places - 1)]
    row_back = [(i + 1, i) for i in range(places - 1)]

    def exchange(value):
        value = value.reshape(slabs * places, 1, chunk)
        value = lax.all_to_all(value, BOTH, split_axis=0, concat_axis=0, tiled=True)
        return value.reshape(packed)

    dual = ()
    total = ()
    for iteration in range(ITERS):
        new_d, new_x, new_y, plane, edge = call(
            functools.partial(prox_body, bool(dual), places - 1),
            [field] * 3 + edges, scalars=1, n_in=3 + len(dual), cost=(density.size * 200, 8 * nbytes), name="prox",
        )(place, density, flux_x, flux_y, *dual)
        plane = lax.ppermute(plane, "tm", loop_next)
        edge = lax.ppermute(edge, "space", row_next)
        (modes,) = call(
            functools.partial(forward_body, places - 1), [packed],
            scratch=[pltpu.VMEM((steps * rows, width), bf16)] * 2, scalars=1, n_in=11, cost=(mega, 9 * nbytes), name="forward",
        )(place, density, flux_x, flux_y, new_d, new_x, new_y, source, plane, edge, ch, cl)
        modes = exchange(modes)
        modes, solved = call(
            functools.partial(solve_body, slabs, places, steps, bool(total)),
            [packed, (2 * length, width)], scratch=[pltpu.VMEM((2 * length, width), f32)],
            n_in=8 + len(total), cost=(3 * mega, 6 * nbytes), name="solve",
        )(modes, ch, cl, wh, wl, vh, vl, den, *total)
        total = (solved,)
        modes = exchange(modes)
        update, plane, edge = call(
            backward_body, [field] + edges, n_in=3, cost=(mega, 3 * nbytes), name="backward",
        )(modes, ch, cl)
        density, flux_x, flux_y = new_d, new_x, new_y
        if iteration + 1 < ITERS:
            dual = (update, lax.ppermute(plane, "tm", loop_back), lax.ppermute(edge, "space", row_back))
    return density, flux_x, flux_y, update


def solution(mesh):
    spec = P("tm", "space", None)
    return jax.shard_map(local, mesh=mesh, in_specs=(spec,) * 4, out_specs=(spec,) * 4, check_vma=False)
```

```python
import functools

import jax
import jax.numpy as jnp
import numpy as np
from jax import lax
from jax.experimental import pallas as pl
from jax.experimental.pallas import tpu as pltpu
from jax.sharding import PartitionSpec as P

ITERS = 3
NEWTON = 10
TAU_STEP = 1.0
SLOW_LOOP = 2.25
INTERPRET = False
BOTH = ("tm", "space")
f32 = jnp.float32
bf16 = jnp.bfloat16
NN = (((1,), (0,)), ((), ()))
NT = (((1,), (1,)), ((), ()))
TN = (((0,), (0,)), ((), ()))


def halves(value):
    high = value.astype(bf16)
    return high, (value - high.astype(f32)).astype(bf16)


def dot3(left, right, dims):
    dot = functools.partial(lax.dot_general, dimension_numbers=dims, preferred_element_type=f32)
    return dot(left[0], right[0]) + (dot(left[0], right[1]) + dot(left[1], right[0]))


def cosine_matrix(points):
    one = np.float32
    frequency = np.arange(points, dtype=one)[:, None]
    sample = np.arange(points, dtype=one)[None, :]
    scaling = np.where(frequency == 0, np.sqrt(one(1.0 / points)), np.sqrt(one(2.0 / points))).astype(one)
    angle = one(np.pi) * (sample + one(0.5)) * frequency / one(points)
    return (scaling * np.cos(angle.astype(np.float64)).astype(one)).astype(one)


def neumann_spectrum(points):
    half_angle = np.pi * np.arange(points) / (2.0 * points)
    return (4.0 * np.sin(half_angle) ** 2).astype(np.float32)


def loop_basis(length, slabs):
    rows = [np.full(length, np.sqrt(1.0 / length))]
    values = [0.0]
    moment = np.arange(length)
    for k in range(1, length // 2):
        angle = 2.0 * np.pi * ((k * moment) % length) / length
        rows += [np.sqrt(2.0 / length) * np.cos(angle), np.sqrt(2.0 / length) * np.sin(angle)]
        values += [4.0 * np.sin(np.pi * k / length) ** 2] * 2
    rows.append(np.sqrt(1.0 / length) * (-1.0) ** moment)
    values.append(4.0)
    basis = np.stack(rows).reshape(length, slabs, length // slabs).transpose(0, 2, 1).reshape(length, length)
    return basis.astype(np.float32), np.asarray(values, np.float32)


def np_halves(matrix):
    high = matrix.astype(bf16)
    return high, (matrix - high.astype(np.float32)).astype(bf16)


def call(body, outs, scratch=(), scalars=0, n_in=0, cost=None, **kw):
    vmem = pl.BlockSpec(memory_space=pltpu.VMEM)
    smem = pl.BlockSpec(memory_space=pltpu.SMEM)
    return pl.pallas_call(
        body,
        out_shape=[jax.ShapeDtypeStruct(s, f32) for s in outs],
        in_specs=[smem] * scalars + [vmem] * n_in,
        out_specs=[vmem] * len(outs),
        scratch_shapes=list(scratch),
        cost_estimate=pl.CostEstimate(flops=int(cost[0]), bytes_accessed=int(cost[1]), transcendentals=0),
        interpret=INTERPRET,
        **kw,
    )


def newton(mass, along_x, along_y):
    target = 0.5 * TAU_STEP * (along_x * along_x + along_y * along_y)
    root = jnp.maximum(mass, 0.0) + jnp.exp(jnp.log(target) * (1.0 / 3.0))
    shifted = root + TAU_STEP
    base = mass + TAU_STEP
    base_twice = base + base
    for _ in range(NEWTON):
        twice = shifted + shifted
        above = (shifted * shifted) * (twice - base) + target
        below = shifted * ((twice + shifted) - base_twice)
        shifted = jnp.maximum(above / below, TAU_STEP)
    root = shifted - TAU_STEP
    factor = root / shifted
    return root, factor * along_x, factor * along_y


def prox_cells(source, result):
    steps, rows, width = result[0].shape
    chunk = 16
    per = rows // chunk

    def step(index, carry):
        t = index // per
        span = pl.ds(pl.multiple_of((index % per) * chunk, chunk), chunk)
        out = newton(*[ref[t, span, :] for ref in source])
        for ref, value in zip(result, out):
            ref[t, span, :] = value
        return carry

    lax.fori_loop(0, steps * per, step, 0)


def transform_back(y, ch, cl, u, pairs, group):
    cosine = (ch[...], cl[...])
    count = y.shape[0] // group
    lanes = y.shape[1]
    for pair in range(pairs):
        even = y[pl.ds(pair, count, stride=group), :]
        odd = y[pl.ds(group // 2 + pair, count, stride=group), :]
        u[pair * lanes : (pair + 1) * lanes, :] = dot3(halves(jnp.concatenate([even, odd], axis=0)), cosine, TN)


def dual_step(d, fx, fy, edge, u, nd, nx, ny):
    steps, rows, width = d.shape
    below_at = (steps + 1) * rows
    above_at = below_at + 8
    end_row = lax.broadcasted_iota(jnp.int32, (rows, width), 0) == rows - 1
    end_column = lax.broadcasted_iota(jnp.int32, (rows, width), 1) == width - 1
    for t in range(steps):
        here = u[t * rows : (t + 1) * rows, :]
        later = u[(t + 1) * rows : (t + 2) * rows, :]
        below = jnp.where(end_row, u[below_at + t : below_at + t + 1, :], pltpu.roll(here, rows - 1, 0))
        right = jnp.where(end_column, here, pltpu.roll(here, width - 1, 1))
        nd[t] = d[t] - TAU_STEP * (here - later)
        nx[t] = fx[t] - TAU_STEP * (here - below)
        ny[t] = fy[t] - TAU_STEP * (here - right)
    here = u[above_at : above_at + steps, :]
    later = u[above_at + 1 : above_at + 1 + steps, :]
    below = jnp.concatenate([u[t * rows : t * rows + 1, :] for t in range(steps)], axis=0)
    right = jnp.where(end_column[:steps, :], here, pltpu.roll(here, width - 1, 1))
    return (
        edge[0] - TAU_STEP * (here - later),
        edge[1] - TAU_STEP * (here - below),
        edge[2] - TAU_STEP * (here - right),
    )


def residual_modes(place, last_place, d, fx, fy, nd, nx, ny, src, edge_x, new_edge_x, ch, cl, out, rh, rl):
    steps, rows, width = d.shape
    shape = (rows, width)
    row = lax.broadcasted_iota(jnp.int32, shape, 0)
    column = lax.broadcasted_iota(jnp.int32, shape, 1)
    final_row = (row == rows - 1) & (place == last_place)
    edge_bar = jnp.where(place == 0, 0.0, 2.0 * new_edge_x - edge_x)
    before = None
    for t in range(steps):
        mass = 2.0 * nd[t] - d[t]
        along_x = 2.0 * nx[t] - fx[t]
        along_y = 2.0 * ny[t] - fy[t]
        x_before = jnp.where(row == 0, edge_bar[t : t + 1, :], pltpu.roll(along_x, 1, 0))
        y_before = jnp.where(column == 0, 0.0, pltpu.roll(along_y, 1, 1))
        value = mass if before is None else mass - before
        value = value + (jnp.where(final_row, 0.0, along_x) - x_before)
        value = value + (jnp.where(column == width - 1, 0.0, along_y) - y_before)
        value = value - src[t]
        before = mass
        high, low = halves(value)
        rh[t * rows : (t + 1) * rows, :] = high
        rl[t * rows : (t + 1) * rows, :] = low
    high, low = halves(before)
    for t in (steps, steps + 1):
        rh[t * rows : (t + 1) * rows, :] = high
        rl[t * rows : (t + 1) * rows, :] = low
    modes = dot3((ch[...], cl[...]), (rh[...], rl[...]), NT)
    lanes = 2 * rows
    pairs = steps // 2
    count = width // 2
    group = 2 * pairs + 1
    for pair in range(pairs):
        span = slice(pair * lanes, (pair + 1) * lanes)
        out[pl.ds(pair, count, stride=group), :] = modes[:count, span]
        out[pl.ds(pairs + pair, count, stride=group), :] = modes[count:, span]
    span = slice(pairs * lanes, (pairs + 1) * lanes)
    low_half = lax.broadcasted_iota(jnp.int32, (count, lanes), 1) < rows
    out[pl.ds(2 * pairs, count, stride=group), :] = jnp.where(low_half, modes[:count, span], modes[count:, span])


def prox_body(d, fx, fy, nd, nx, ny):
    prox_cells((d, fx, fy), (nd, nx, ny))


def forward_body(last_place, place, d, fx, fy, nd, nx, ny, src, edge, ch, cl, out, new_edge, rh, rl):
    fresh = newton(edge[0], edge[1], edge[2])
    for k in range(3):
        new_edge[k] = fresh[k]
    residual_modes(place[0], last_place, d, fx, fy, nd, nx, ny, src, edge[1], fresh[1], ch, cl, out, rh, rl)


def middle_body(last_place, place, y, d, fx, fy, src, edge, ch, cl, nd, nx, ny, out, new_edge, u, rh, rl):
    steps = d.shape[0]
    pairs = steps // 2 + 1
    transform_back(y, ch, cl, u, pairs, 2 * pairs)
    fresh = newton(*dual_step(d, fx, fy, edge, u, nd, nx, ny))
    for k in range(3):
        new_edge[k] = fresh[k]
    prox_cells((nd, nx, ny), (nd, nx, ny))
    residual_modes(place[0], last_place, d, fx, fy, nd, nx, ny, src, edge[1], fresh[1], ch, cl, out, rh, rl)


def last_body(y, ch, cl, u, flat):
    steps, rows, _ = u.shape
    transform_back(y, ch, cl, flat, steps // 2, steps)
    for t in range(steps):
        u[t] = flat[t * rows : (t + 1) * rows, :]


def solve_body(slabs, places, steps, with_sum, with_edges, *refs):
    if with_sum:
        z, ch, cl, wh, wl, vh, vl, den, so_far, out, total, field = refs
    else:
        z, ch, cl, wh, wl, vh, vl, den, out, total, field = refs
    length = slabs * steps
    pairs = steps // 2
    lanes = z.shape[1]
    rows = lanes // 2
    lane = lax.broadcasted_iota(jnp.int32, (slabs, lanes), 1)
    low_half = lane < rows

    def swap(a, b):
        return jnp.where(low_half, a, pltpu.roll(b, rows, 1)), jnp.where(low_half, pltpu.roll(a, rows, 1), b)

    group = 2 * pairs + 1

    def arrived(place, item):
        return z[pl.ds(place * group + item, slabs, stride=places * group), :]

    for q in range(places // 2):
        span = slice(q * lanes, (q + 1) * lanes)
        planes = swap(arrived(2 * q, 2 * pairs), arrived(2 * q + 1, 2 * pairs))
        for mode in range(2):
            for pair in range(pairs):
                item = mode * pairs + pair
                first, second = swap(arrived(2 * q, item), arrived(2 * q + 1, item))
                if pair == 0:
                    first = first - pltpu.roll(planes[mode], 1, 0)
                top = mode * length + 2 * pair * slabs
                field[top : top + slabs, span] = first
                field[top + slabs : top + 2 * slabs, span] = second
    cosine = (ch[...], cl[...])
    for mode in range(2):
        span = slice(mode * length, (mode + 1) * length)
        field[span, :] = dot3((wh[...], wl[...]), halves(field[span, :]), NN)
    solved = dot3(halves(field[...]), cosine, NT) / den[...]
    if with_sum:
        solved = solved + so_far[...]
    total[...] = solved
    field[...] = dot3(halves(solved), cosine, NN)
    for mode in range(2):
        span = slice(mode * length, (mode + 1) * length)
        field[span, :] = dot3((vh[...], vl[...]), halves(field[span, :]), NN)
    per_mode = pairs + 1 if with_edges else pairs
    group_out = 2 * per_mode

    def leaving(place, item):
        return pl.ds(place * group_out + item, slabs, stride=places * group_out)

    for mode in range(2):
        top = mode * length
        for q in range(places // 2):
            span = slice(q * lanes, (q + 1) * lanes)
            for pair in range(pairs):
                at = top + 2 * pair * slabs
                first, second = swap(field[at : at + slabs, span], field[at + slabs : at + 2 * slabs, span])
                out[leaving(2 * q, mode * per_mode + pair), :] = first
                out[leaving(2 * q + 1, mode * per_mode + pair), :] = second
            if not with_edges:
                continue
            ahead = pltpu.roll(field[top : top + slabs, span], slabs - 1, 0)
            for place, value in ((2 * q, ahead), (2 * q + 1, pltpu.roll(ahead, rows, 1))):
                after = (place + 1) * rows if place + 1 < places else (place + 1) * rows - 1
                for t in range(steps):
                    column = field[top + t * slabs : top + (t + 1) * slabs, after : after + 1]
                    value = jnp.where(lane == rows + t, column, value)
                if place:
                    before = place * rows - 1
                    for t in range(steps + 1):
                        column = field[top + (t % steps) * slabs : top + (t % steps + 1) * slabs, before : before + 1]
                        if t == steps:
                            column = pltpu.roll(jnp.broadcast_to(column, (slabs, lanes)), slabs - 1, 0)
                        value = jnp.where(lane == rows + 8 + t, column, value)
                out[leaving(place, mode * per_mode + pairs), :] = value


def local(density, flux_x, flux_y, source):
    steps, rows, width = density.shape
    slabs = lax.axis_size("tm")
    places = lax.axis_size("space")
    length = steps * slabs
    screen = SLOW_LOOP / float(length * length)
    order = np.concatenate([np.arange(0, width, 2), np.arange(1, width, 2)])
    ch, cl = (jnp.asarray(m) for m in np_halves(cosine_matrix(width)[order]))
    basis, loop_values = loop_basis(length, slabs)
    wh, wl = (jnp.asarray(m) for m in np_halves(basis))
    vh, vl = (jnp.asarray(m) for m in np_halves(np.ascontiguousarray(basis.T)))
    spectrum = neumann_spectrum(width)
    place = lax.axis_index("space")
    first = 2 * (lax.axis_index("tm") * places + place)
    own = lax.dynamic_slice_in_dim(jnp.asarray(spectrum), first, 2)
    den = own[:, None, None] + jnp.asarray(loop_values)[None, :, None] + jnp.asarray(spectrum[order])[None, None, :]
    den = (den + screen).reshape(2 * length, width)
    place = place.astype(jnp.int32).reshape(1)
    nbytes = density.size * 4
    mega = density.size * width * 6
    field = (steps, rows, width)
    edge_shape = (3, steps, width)
    lanes = 2 * rows
    devices = slabs * places

    def packed(items):
        return (devices * items, lanes)

    forward_items = steps + 1
    backward_items = steps + 2

    def exchange(value):
        shape = value.shape
        value = value.reshape(devices, 1, shape[0] // devices * lanes)
        value = lax.all_to_all(value, BOTH, split_axis=0, concat_axis=0, tiled=True)
        return value.reshape(shape)

    edge = jnp.stack([density[:, rows - 1], flux_x[:, rows - 1], flux_y[:, rows - 1]])
    edge = lax.ppermute(edge, "space", [(i, i + 1) for i in range(places - 1)])
    split = [pltpu.VMEM(((steps + 2) * rows, width), bf16)] * 2
    new_d, new_x, new_y = call(
        prox_body, [field] * 3, n_in=3, cost=(density.size * 200, 6 * nbytes), name="prox"
    )(density, flux_x, flux_y)
    modes, edge = call(
        functools.partial(forward_body, places - 1), [packed(forward_items), edge_shape],
        scratch=split, scalars=1, n_in=10, cost=(mega, 8 * nbytes), name="forward",
    )(place, density, flux_x, flux_y, new_d, new_x, new_y, source, edge, ch, cl)
    density, flux_x, flux_y = new_d, new_x, new_y
    total = ()
    for iteration in range(ITERS):
        final = iteration + 1 == ITERS
        modes = exchange(modes)
        modes, solved = call(
            functools.partial(solve_body, slabs, places, steps, bool(total), not final),
            [packed(steps if final else backward_items), (2 * length, width)],
            scratch=[pltpu.VMEM((2 * length, width), f32)],
            n_in=8 + len(total), cost=(3 * mega, 6 * nbytes), name="solve",
        )(modes, ch, cl, wh, wl, vh, vl, den, *total)
        total = (solved,)
        modes = exchange(modes)
        if final:
            break
        density, flux_x, flux_y, modes, edge = call(
            functools.partial(middle_body, places - 1), [field] * 3 + [packed(forward_items), edge_shape],
            scratch=[pltpu.VMEM(((steps + 2) * rows, width), f32)] + split,
            scalars=1, n_in=8, cost=(2 * mega, 10 * nbytes), name="middle",
        )(place, modes, density, flux_x, flux_y, source, edge, ch, cl)
    (potential,) = call(
        last_body, [field], scratch=[pltpu.VMEM((steps * rows, width), f32)], n_in=3, cost=(mega, 3 * nbytes), name="last"
    )(modes, ch, cl)
    return density, flux_x, flux_y, potential


def solution(mesh):
    spec = P("tm", "space", None)
    return jax.shard_map(local, mesh=mesh, in_specs=(spec,) * 4, out_specs=(spec,) * 4, check_vma=False)
```

```python
import functools

import jax
import jax.numpy as jnp
import numpy as np
from jax import lax
from jax.experimental import pallas as pl
from jax.experimental.pallas import tpu as pltpu
from jax.sharding import PartitionSpec as P

ITERS = 3
NEWTON = 10
TAU_STEP = 1.0
SLOW_LOOP = 2.25
INTERPRET = False
GRANT = 20 << 20
BOTH = ("tm", "space")
f32 = jnp.float32
bf16 = jnp.bfloat16
NN = (((1,), (0,)), ((), ()))
NT = (((1,), (1,)), ((), ()))
TN = (((0,), (0,)), ((), ()))


def halves(value):
    high = value.astype(bf16)
    return high, (value - high.astype(f32)).astype(bf16)


def dot3(left, right, dims):
    dot = functools.partial(lax.dot_general, dimension_numbers=dims, preferred_element_type=f32)
    return dot(left[0], right[0]) + (dot(left[0], right[1]) + dot(left[1], right[0]))


def cosine_matrix(points):
    one = np.float32
    frequency = np.arange(points, dtype=one)[:, None]
    sample = np.arange(points, dtype=one)[None, :]
    scaling = np.where(frequency == 0, np.sqrt(one(1.0 / points)), np.sqrt(one(2.0 / points))).astype(one)
    angle = one(np.pi) * (sample + one(0.5)) * frequency / one(points)
    return (scaling * np.cos(angle.astype(np.float64)).astype(one)).astype(one)


def neumann_spectrum(points):
    half_angle = np.pi * np.arange(points) / (2.0 * points)
    return (4.0 * np.sin(half_angle) ** 2).astype(np.float32)


def loop_basis(length, slabs):
    rows = [np.full(length, np.sqrt(1.0 / length))]
    values = [0.0]
    moment = np.arange(length)
    for k in range(1, length // 2):
        angle = 2.0 * np.pi * ((k * moment) % length) / length
        rows += [np.sqrt(2.0 / length) * np.cos(angle), np.sqrt(2.0 / length) * np.sin(angle)]
        values += [4.0 * np.sin(np.pi * k / length) ** 2] * 2
    rows.append(np.sqrt(1.0 / length) * (-1.0) ** moment)
    values.append(4.0)
    basis = np.stack(rows).reshape(length, slabs, length // slabs).transpose(0, 2, 1).reshape(length, length)
    return basis.astype(np.float32), np.asarray(values, np.float32)


def np_halves(matrix):
    high = matrix.astype(bf16)
    return high, (matrix - high.astype(np.float32)).astype(bf16)


def call(body, outs, scratch=(), scalars=0, n_in=0, cost=None, **kw):
    vmem = pl.BlockSpec(memory_space=pltpu.VMEM)
    smem = pl.BlockSpec(memory_space=pltpu.SMEM)
    return pl.pallas_call(
        body,
        out_shape=[pltpu.VMEM(s, f32) for s in outs],
        in_specs=[smem] * scalars + [vmem] * n_in,
        out_specs=[vmem] * len(outs),
        scratch_shapes=list(scratch),
        cost_estimate=pl.CostEstimate(flops=int(cost[0]), bytes_accessed=int(cost[1]), transcendentals=0),
        interpret=INTERPRET,
        compiler_params=pltpu.CompilerParams(vmem_limit_bytes=GRANT),
        **kw,
    )


def newton(mass, along_x, along_y):
    target = 0.5 * TAU_STEP * (along_x * along_x + along_y * along_y)
    root = jnp.maximum(mass, 0.0) + jnp.exp(jnp.log(target) * (1.0 / 3.0))
    shifted = root + TAU_STEP
    base = mass + TAU_STEP
    base_twice = base + base
    for _ in range(NEWTON):
        twice = shifted + shifted
        above = (shifted * shifted) * (twice - base) + target
        below = shifted * ((twice + shifted) - base_twice)
        shifted = jnp.maximum(above / below, TAU_STEP)
    root = shifted - TAU_STEP
    factor = root / shifted
    return root, factor * along_x, factor * along_y


def prox_cells(source, result):
    steps, rows, width = result[0].shape
    chunk = 16
    per = rows // chunk

    def step(index, carry):
        t = index // per
        span = pl.ds(pl.multiple_of((index % per) * chunk, chunk), chunk)
        out = newton(*[ref[t, span, :] for ref in source])
        for ref, value in zip(result, out):
            ref[t, span, :] = value
        return carry

    lax.fori_loop(0, steps * per, step, 0)


def transform_back(y, ch, cl, u, pairs, group):
    cosine = (ch[...], cl[...])
    count = y.shape[0] // group
    lanes = y.shape[1]
    for pair in range(pairs):
        even = y[pl.ds(pair, count, stride=group), :]
        odd = y[pl.ds(group // 2 + pair, count, stride=group), :]
        u[pair * lanes : (pair + 1) * lanes, :] = dot3(halves(jnp.concatenate([even, odd], axis=0)), cosine, TN)


def dual_step(d, fx, fy, edge, u, nd, nx, ny):
    steps, rows, width = d.shape
    below_at = (steps + 1) * rows
    above_at = below_at + 8
    end_row = lax.broadcasted_iota(jnp.int32, (rows, width), 0) == rows - 1
    end_column = lax.broadcasted_iota(jnp.int32, (rows, width), 1) == width - 1
    for t in range(steps):
        here = u[t * rows : (t + 1) * rows, :]
        later = u[(t + 1) * rows : (t + 2) * rows, :]
        below = jnp.where(end_row, u[below_at + t : below_at + t + 1, :], pltpu.roll(here, rows - 1, 0))
        right = jnp.where(end_column, here, pltpu.roll(here, width - 1, 1))
        nd[t] = d[t] - TAU_STEP * (here - later)
        nx[t] = fx[t] - TAU_STEP * (here - below)
        ny[t] = fy[t] - TAU_STEP * (here - right)
    here = u[above_at : above_at + steps, :]
    later = u[above_at + 1 : above_at + 1 + steps, :]
    below = jnp.concatenate([u[t * rows : t * rows + 1, :] for t in range(steps)], axis=0)
    right = jnp.where(end_column[:steps, :], here, pltpu.roll(here, width - 1, 1))
    return (
        edge[0] - TAU_STEP * (here - later),
        edge[1] - TAU_STEP * (here - below),
        edge[2] - TAU_STEP * (here - right),
    )


def residual_modes(place, last_place, d, fx, fy, nd, nx, ny, src, edge_x, new_edge_x, ch, cl, out, rh, rl):
    steps, rows, width = d.shape
    shape = (rows, width)
    row = lax.broadcasted_iota(jnp.int32, shape, 0)
    column = lax.broadcasted_iota(jnp.int32, shape, 1)
    final_row = (row == rows - 1) & (place == last_place)
    edge_bar = jnp.where(place == 0, 0.0, 2.0 * new_edge_x - edge_x)
    before = None
    for t in range(steps):
        mass = 2.0 * nd[t] - d[t]
        along_x = 2.0 * nx[t] - fx[t]
        along_y = 2.0 * ny[t] - fy[t]
        x_before = jnp.where(row == 0, edge_bar[t : t + 1, :], pltpu.roll(along_x, 1, 0))
        y_before = jnp.where(column == 0, 0.0, pltpu.roll(along_y, 1, 1))
        value = mass if before is None else mass - before
        value = value + (jnp.where(final_row, 0.0, along_x) - x_before)
        value = value + (jnp.where(column == width - 1, 0.0, along_y) - y_before)
        value = value - src[t]
        before = mass
        high, low = halves(value)
        rh[t * rows : (t + 1) * rows, :] = high
        rl[t * rows : (t + 1) * rows, :] = low
    high, low = halves(before)
    for t in (steps, steps + 1):
        rh[t * rows : (t + 1) * rows, :] = high
        rl[t * rows : (t + 1) * rows, :] = low
    modes = dot3((ch[...], cl[...]), (rh[...], rl[...]), NT)
    lanes = 2 * rows
    pairs = steps // 2
    count = width // 2
    group = 2 * pairs + 1
    for pair in range(pairs):
        span = slice(pair * lanes, (pair + 1) * lanes)
        out[pl.ds(pair, count, stride=group), :] = modes[:count, span]
        out[pl.ds(pairs + pair, count, stride=group), :] = modes[count:, span]
    span = slice(pairs * lanes, (pairs + 1) * lanes)
    low_half = lax.broadcasted_iota(jnp.int32, (count, lanes), 1) < rows
    out[pl.ds(2 * pairs, count, stride=group), :] = jnp.where(low_half, modes[:count, span], modes[count:, span])


def edge_body(d, fx, fy, edge):
    rows = d.shape[1]
    for k, ref in enumerate((d, fx, fy)):
        for t in range(d.shape[0]):
            edge[k, t : t + 1, :] = ref[t, rows - 1 :, :]


def last_rows(density, flux_x, flux_y):
    steps, rows, width = density.shape
    block = pl.BlockSpec((steps, 8, width), lambda i: (0, rows // 8 - 1, 0))
    return pl.pallas_call(
        edge_body,
        grid=(1,),
        out_shape=jax.ShapeDtypeStruct((3, steps, width), f32),
        in_specs=[block] * 3,
        out_specs=pl.BlockSpec((3, steps, width), lambda i: (0, 0, 0)),
        compiler_params=pltpu.CompilerParams(vmem_limit_bytes=GRANT),
        interpret=INTERPRET,
        name="edges",
    )(density, flux_x, flux_y)


def prox_body(d, fx, fy, nd, nx, ny):
    prox_cells((d, fx, fy), (nd, nx, ny))


def forward_body(last_place, place, d, fx, fy, nd, nx, ny, src, edge, ch, cl, out, new_edge, rh, rl):
    fresh = newton(edge[0], edge[1], edge[2])
    for k in range(3):
        new_edge[k] = fresh[k]
    residual_modes(place[0], last_place, d, fx, fy, nd, nx, ny, src, edge[1], fresh[1], ch, cl, out, rh, rl)


def middle_body(last_place, place, y, d, fx, fy, src, edge, ch, cl, nd, nx, ny, out, new_edge, u, rh, rl):
    steps = d.shape[0]
    pairs = steps // 2 + 1
    transform_back(y, ch, cl, u, pairs, 2 * pairs)
    fresh = newton(*dual_step(d, fx, fy, edge, u, nd, nx, ny))
    for k in range(3):
        new_edge[k] = fresh[k]
    prox_cells((nd, nx, ny), (nd, nx, ny))
    residual_modes(place[0], last_place, d, fx, fy, nd, nx, ny, src, edge[1], fresh[1], ch, cl, out, rh, rl)


def last_body(y, ch, cl, u, flat):
    steps, rows, _ = u.shape
    transform_back(y, ch, cl, flat, steps // 2, steps)
    for t in range(steps):
        u[t] = flat[t * rows : (t + 1) * rows, :]


def solve_body(slabs, places, steps, with_sum, with_edges, *refs):
    if with_sum:
        z, ch, cl, wh, wl, vh, vl, den, so_far, out, total, field = refs
    else:
        z, ch, cl, wh, wl, vh, vl, den, out, total, field = refs
    length = slabs * steps
    pairs = steps // 2
    lanes = z.shape[1]
    rows = lanes // 2
    lane = lax.broadcasted_iota(jnp.int32, (slabs, lanes), 1)
    low_half = lane < rows

    def swap(a, b):
        return jnp.where(low_half, a, pltpu.roll(b, rows, 1)), jnp.where(low_half, pltpu.roll(a, rows, 1), b)

    group = 2 * pairs + 1

    def arrived(place, item):
        return z[pl.ds(place * group + item, slabs, stride=places * group), :]

    for q in range(places // 2):
        span = slice(q * lanes, (q + 1) * lanes)
        planes = swap(arrived(2 * q, 2 * pairs), arrived(2 * q + 1, 2 * pairs))
        for mode in range(2):
            for pair in range(pairs):
                item = mode * pairs + pair
                first, second = swap(arrived(2 * q, item), arrived(2 * q + 1, item))
                if pair == 0:
                    first = first - pltpu.roll(planes[mode], 1, 0)
                top = mode * length + 2 * pair * slabs
                field[top : top + slabs, span] = first
                field[top + slabs : top + 2 * slabs, span] = second
    cosine = (ch[...], cl[...])
    for mode in range(2):
        span = slice(mode * length, (mode + 1) * length)
        field[span, :] = dot3((wh[...], wl[...]), halves(field[span, :]), NN)
    solved = dot3(halves(field[...]), cosine, NT) / den[...]
    if with_sum:
        solved = solved + so_far[...]
    total[...] = solved
    field[...] = dot3(halves(solved), cosine, NN)
    for mode in range(2):
        span = slice(mode * length, (mode + 1) * length)
        field[span, :] = dot3((vh[...], vl[...]), halves(field[span, :]), NN)
    per_mode = pairs + 1 if with_edges else pairs
    group_out = 2 * per_mode

    def leaving(place, item):
        return pl.ds(place * group_out + item, slabs, stride=places * group_out)

    for mode in range(2):
        top = mode * length
        for q in range(places // 2):
            span = slice(q * lanes, (q + 1) * lanes)
            for pair in range(pairs):
                at = top + 2 * pair * slabs
                first, second = swap(field[at : at + slabs, span], field[at + slabs : at + 2 * slabs, span])
                out[leaving(2 * q, mode * per_mode + pair), :] = first
                out[leaving(2 * q + 1, mode * per_mode + pair), :] = second
            if not with_edges:
                continue
            ahead = pltpu.roll(field[top : top + slabs, span], slabs - 1, 0)
            for place, value in ((2 * q, ahead), (2 * q + 1, pltpu.roll(ahead, rows, 1))):
                after = (place + 1) * rows if place + 1 < places else (place + 1) * rows - 1
                for t in range(steps):
                    column = field[top + t * slabs : top + (t + 1) * slabs, after : after + 1]
                    value = jnp.where(lane == rows + t, column, value)
                if place:
                    before = place * rows - 1
                    for t in range(steps + 1):
                        column = field[top + (t % steps) * slabs : top + (t % steps + 1) * slabs, before : before + 1]
                        if t == steps:
                            column = pltpu.roll(jnp.broadcast_to(column, (slabs, lanes)), slabs - 1, 0)
                        value = jnp.where(lane == rows + 8 + t, column, value)
                out[leaving(place, mode * per_mode + pairs), :] = value


def local(density, flux_x, flux_y, source):
    steps, rows, width = density.shape
    slabs = lax.axis_size("tm")
    places = lax.axis_size("space")
    length = steps * slabs
    screen = SLOW_LOOP / float(length * length)
    order = np.concatenate([np.arange(0, width, 2), np.arange(1, width, 2)])
    ch, cl = (jnp.asarray(m) for m in np_halves(cosine_matrix(width)[order]))
    basis, loop_values = loop_basis(length, slabs)
    wh, wl = (jnp.asarray(m) for m in np_halves(basis))
    vh, vl = (jnp.asarray(m) for m in np_halves(np.ascontiguousarray(basis.T)))
    spectrum = neumann_spectrum(width)
    place = lax.axis_index("space")
    first = 2 * (lax.axis_index("tm") * places + place)
    own = lax.dynamic_slice_in_dim(jnp.asarray(spectrum), first, 2)
    den = own[:, None, None] + jnp.asarray(loop_values)[None, :, None] + jnp.asarray(spectrum[order])[None, None, :]
    den = (den + screen).reshape(2 * length, width)
    place = place.astype(jnp.int32).reshape(1)
    nbytes = density.size * 4
    mega = density.size * width * 6
    field = (steps, rows, width)
    edge_shape = (3, steps, width)
    lanes = 2 * rows
    devices = slabs * places

    def packed(items):
        return (devices * items, lanes)

    forward_items = steps + 1
    backward_items = steps + 2

    def exchange(value):
        shape = value.shape
        value = value.reshape(devices, 1, shape[0] // devices * lanes)
        value = lax.all_to_all(value, BOTH, split_axis=0, concat_axis=0, tiled=True)
        return value.reshape(shape)

    edge = lax.ppermute(last_rows(density, flux_x, flux_y), "space", [(i, i + 1) for i in range(places - 1)])
    split = [pltpu.VMEM(((steps + 2) * rows, width), bf16)] * 2
    new_d, new_x, new_y = call(
        prox_body, [field] * 3, n_in=3, cost=(density.size * 200, 6 * nbytes), name="prox"
    )(density, flux_x, flux_y)
    modes, edge = call(
        functools.partial(forward_body, places - 1), [packed(forward_items), edge_shape],
        scratch=split, scalars=1, n_in=10, cost=(mega, 8 * nbytes), name="forward",
    )(place, density, flux_x, flux_y, new_d, new_x, new_y, source, edge, ch, cl)
    density, flux_x, flux_y = new_d, new_x, new_y
    total = ()
    for iteration in range(ITERS):
        final = iteration + 1 == ITERS
        modes = exchange(modes)
        modes, solved = call(
            functools.partial(solve_body, slabs, places, steps, bool(total), not final),
            [packed(steps if final else backward_items), (2 * length, width)],
            scratch=[pltpu.VMEM((2 * length, width), f32)],
            n_in=8 + len(total), cost=(3 * mega, 6 * nbytes), name="solve",
        )(modes, ch, cl, wh, wl, vh, vl, den, *total)
        total = (solved,)
        modes = exchange(modes)
        if final:
            break
        density, flux_x, flux_y, modes, edge = call(
            functools.partial(middle_body, places - 1), [field] * 3 + [packed(forward_items), edge_shape],
            scratch=[pltpu.VMEM(((steps + 2) * rows, width), f32)] + split,
            scalars=1, n_in=8, cost=(2 * mega, 10 * nbytes), name="middle",
        )(place, modes, density, flux_x, flux_y, source, edge, ch, cl)
    (potential,) = call(
        last_body, [field], scratch=[pltpu.VMEM((steps * rows, width), f32)], n_in=3, cost=(mega, 3 * nbytes), name="last"
    )(modes, ch, cl)
    return density, flux_x, flux_y, potential


def solution(mesh):
    spec = P("tm", "space", None)
    return jax.shard_map(local, mesh=mesh, in_specs=(spec,) * 4, out_specs=(spec,) * 4, check_vma=False)
```

```python
import functools

import jax
import jax.numpy as jnp
import numpy as np
from jax import lax
from jax.experimental import pallas as pl
from jax.experimental.pallas import tpu as pltpu
from jax.sharding import PartitionSpec as P

ITERS = 3
NEWTON = 10
TAU_STEP = 1.0
SLOW_LOOP = 2.25
INTERPRET = False
GRANT = 20 << 20
KEPT = 8
TAKEN = 9
BLOCK = 16
BOTH = ("tm", "space")
f32 = jnp.float32
bf16 = jnp.bfloat16
NN = (((1,), (0,)), ((), ()))
NT = (((1,), (1,)), ((), ()))
TN = (((0,), (0,)), ((), ()))


def halves(value):
    high = value.astype(bf16)
    return high, (value - high.astype(f32)).astype(bf16)


def dot3(left, right, dims):
    dot = functools.partial(lax.dot_general, dimension_numbers=dims, preferred_element_type=f32)
    return dot(left[0], right[0]) + (dot(left[0], right[1]) + dot(left[1], right[0]))


def cosine_matrix(points):
    one = np.float32
    frequency = np.arange(points, dtype=one)[:, None]
    sample = np.arange(points, dtype=one)[None, :]
    scaling = np.where(frequency == 0, np.sqrt(one(1.0 / points)), np.sqrt(one(2.0 / points))).astype(one)
    angle = one(np.pi) * (sample + one(0.5)) * frequency / one(points)
    return (scaling * np.cos(angle.astype(np.float64)).astype(one)).astype(one)


def neumann_spectrum(points):
    half_angle = np.pi * np.arange(points) / (2.0 * points)
    return (4.0 * np.sin(half_angle) ** 2).astype(np.float32)


def loop_basis(length, slabs):
    rows = [np.full(length, np.sqrt(1.0 / length))]
    values = [0.0]
    moment = np.arange(length)
    for k in range(1, length // 2):
        angle = 2.0 * np.pi * ((k * moment) % length) / length
        rows += [np.sqrt(2.0 / length) * np.cos(angle), np.sqrt(2.0 / length) * np.sin(angle)]
        values += [4.0 * np.sin(np.pi * k / length) ** 2] * 2
    rows.append(np.sqrt(1.0 / length) * (-1.0) ** moment)
    values.append(4.0)
    basis = np.stack(rows).reshape(length, slabs, length // slabs).transpose(0, 2, 1).reshape(length, length)
    return basis.astype(np.float32), np.asarray(values, np.float32)


def np_halves(matrix):
    high = matrix.astype(bf16)
    return high, (matrix - high.astype(np.float32)).astype(bf16)


def call(body, outs, scratch=(), scalars=0, far=0, n_in=0, far_out=False, cost=None, **kw):
    vmem = pl.BlockSpec(memory_space=pltpu.VMEM)
    smem = pl.BlockSpec(memory_space=pltpu.SMEM)
    hbm = pl.BlockSpec(memory_space=pltpu.HBM)
    return pl.pallas_call(
        body,
        out_shape=[jax.ShapeDtypeStruct(s, f32) if far_out else pltpu.VMEM(s, f32) for s in outs],
        in_specs=[smem] * scalars + [hbm] * far + [vmem] * n_in,
        out_specs=[hbm if far_out else vmem] * len(outs),
        scratch_shapes=list(scratch),
        cost_estimate=pl.CostEstimate(flops=int(cost[0]), bytes_accessed=int(cost[1]), transcendentals=0),
        compiler_params=pltpu.CompilerParams(vmem_limit_bytes=GRANT),
        interpret=INTERPRET,
        **kw,
    )


def newton(mass, along_x, along_y):
    target = 0.5 * TAU_STEP * (along_x * along_x + along_y * along_y)
    root = jnp.maximum(mass, 0.0) + jnp.exp(jnp.log(target) * (1.0 / 3.0))
    shifted = root + TAU_STEP
    base = mass + TAU_STEP
    base_twice = base + base
    for _ in range(NEWTON):
        twice = shifted + shifted
        above = (shifted * shifted) * (twice - base) + target
        below = shifted * ((twice + shifted) - base_twice)
        shifted = jnp.maximum(above / below, TAU_STEP)
    root = shifted - TAU_STEP
    factor = root / shifted
    return root, factor * along_x, factor * along_y


def prox_cells(source, result, wait=None):
    steps, rows, width = result[0].shape
    chunk = 32
    per = rows // chunk

    def step(index, carry):
        t = index // per
        if wait is not None:
            pl.when(index % per == 0)(lambda: wait(t))
        span = pl.ds(pl.multiple_of((index % per) * chunk, chunk), chunk)
        out = newton(*[ref[t, span, :] for ref in source])
        for ref, value in zip(result, out):
            ref[t, span, :] = value
        return carry

    lax.fori_loop(0, steps * per, step, 0)


def transform_back(y, ch, cl, u, pair, group, packed_edge=False):
    count = y.shape[0] // group
    lanes = y.shape[1]
    if packed_edge:
        both = y[pl.ds(pair * 2, count, stride=group), :]
        even, odd = both, pltpu.roll(both, lanes // 2, 1)
        kept = lanes // 2
    else:
        even = y[pl.ds(pair, count, stride=group), :]
        odd = y[pl.ds(group // 2 + pair, count, stride=group), :]
        kept = lanes
    value = dot3(halves(jnp.concatenate([even, odd], axis=0)), (ch[...], cl[...]), TN)
    u[pair * lanes : pair * lanes + kept, :] = value[:kept, :]


def fill_plane(u, steps, rows, screen, residual_sum):
    at = (steps - 1) * rows + KEPT
    here = u[at : at + BLOCK, :]
    width = here.shape[1]
    column = lax.broadcasted_iota(jnp.int32, here.shape, 1)
    right = jnp.where(column == width - 1, here, pltpu.roll(here, width - 1, 1))
    left = jnp.where(column == 0, here, pltpu.roll(here, 1, 1))
    earlier = u[at - rows : at - rows + BLOCK, :]
    value = (here - earlier) + (here - u[at - 1 : at - 1 + BLOCK, :]) + (here - u[at + 1 : at + 1 + BLOCK, :])
    value = here + (value + (here - right) + (here - left) + screen * here - residual_sum)
    at = steps * rows + KEPT
    row = lax.broadcasted_iota(jnp.int32, here.shape, 0)
    u[at : at + BLOCK, :] = jnp.where(row < TAKEN, value, u[at : at + BLOCK, :])


def dual_step(d, fx, fy, edge, u, nd, nx, ny):
    steps, rows, width = d.shape
    below_at = (steps + 1) * rows
    above_at = below_at + steps
    end_row = lax.broadcasted_iota(jnp.int32, (rows, width), 0) == rows - 1
    end_column = lax.broadcasted_iota(jnp.int32, (rows, width), 1) == width - 1
    for t in range(steps):
        here = u[t * rows : (t + 1) * rows, :]
        later = u[(t + 1) * rows : (t + 2) * rows, :]
        below = jnp.where(end_row, u[below_at + t : below_at + t + 1, :], pltpu.roll(here, rows - 1, 0))
        right = jnp.where(end_column, here, pltpu.roll(here, width - 1, 1))
        nd[t] = d[t] - TAU_STEP * (here - later)
        nx[t] = fx[t] - TAU_STEP * (here - below)
        ny[t] = fy[t] - TAU_STEP * (here - right)
    here = u[above_at : above_at + steps, :]
    later = u[above_at + 1 : above_at + 1 + steps, :]
    below = jnp.concatenate([u[t * rows : t * rows + 1, :] for t in range(steps)], axis=0)
    right = jnp.where(end_column[:steps, :], here, pltpu.roll(here, width - 1, 1))
    return (
        edge[0] - TAU_STEP * (here - later),
        edge[1] - TAU_STEP * (here - below),
        edge[2] - TAU_STEP * (here - right),
    )


def residual_modes(place, last_place, d, fx, fy, nd, nx, ny, src, edge_x, new_edge_x, ch, cl, out, kept, rh, rl):
    steps, rows, width = d.shape
    shape = (rows, width)
    row = lax.broadcasted_iota(jnp.int32, shape, 0)
    column = lax.broadcasted_iota(jnp.int32, shape, 1)
    final_row = (row == rows - 1) & (place == last_place)
    edge_bar = jnp.where(place == 0, 0.0, 2.0 * new_edge_x - edge_x)
    before = None
    for t in range(steps):
        mass = 2.0 * nd[t] - d[t]
        along_x = 2.0 * nx[t] - fx[t]
        along_y = 2.0 * ny[t] - fy[t]
        x_before = jnp.where(row == 0, edge_bar[t : t + 1, :], pltpu.roll(along_x, 1, 0))
        y_before = jnp.where(column == 0, 0.0, pltpu.roll(along_y, 1, 1))
        value = mass if before is None else mass - before
        value = value + (jnp.where(final_row, 0.0, along_x) - x_before)
        value = value + (jnp.where(column == width - 1, 0.0, along_y) - y_before)
        value = value - src[t]
        before = mass
        high, low = halves(value)
        rh[t * rows : (t + 1) * rows, :] = high
        rl[t * rows : (t + 1) * rows, :] = low
    kept[...] = value[KEPT : KEPT + BLOCK, :]
    high, low = halves(before)
    for t in (steps, steps + 1):
        rh[t * rows : (t + 1) * rows, :] = high
        rl[t * rows : (t + 1) * rows, :] = low
    modes = dot3((ch[...], cl[...]), (rh[...], rl[...]), NT)
    lanes = 2 * rows
    pairs = steps // 2
    count = width // 2
    group = 2 * pairs + 1
    for pair in range(pairs):
        span = slice(pair * lanes, (pair + 1) * lanes)
        out[pl.ds(pair, count, stride=group), :] = modes[:count, span]
        out[pl.ds(pairs + pair, count, stride=group), :] = modes[count:, span]
    span = slice(pairs * lanes, (pairs + 1) * lanes)
    low_half = lax.broadcasted_iota(jnp.int32, (count, lanes), 1) < rows
    out[pl.ds(2 * pairs, count, stride=group), :] = jnp.where(low_half, modes[:count, span], modes[count:, span])


def edge_body(d, fx, fy, edge):
    rows = d.shape[1]
    for k, ref in enumerate((d, fx, fy)):
        for t in range(d.shape[0]):
            edge[k, t : t + 1, :] = ref[t, rows - 1 :, :]


def stay(value):
    return value if INTERPRET else pltpu.with_memory_space_constraint(value, pltpu.HBM)


def last_rows(density, flux_x, flux_y):
    steps, rows, width = density.shape
    block = pl.BlockSpec((steps, 8, width), lambda i: (0, rows // 8 - 1, 0))
    return pl.pallas_call(
        edge_body,
        grid=(1,),
        out_shape=jax.ShapeDtypeStruct((3, steps, width), f32),
        in_specs=[block] * 3,
        out_specs=pl.BlockSpec((3, steps, width), lambda i: (0, 0, 0)),
        compiler_params=pltpu.CompilerParams(vmem_limit_bytes=GRANT),
        interpret=INTERPRET,
        name="edges",
    )(*map(stay, (density, flux_x, flux_y)))


def prox_body(d, fx, fy, nd, nx, ny, own_d, own_x, own_y, sems):
    steps = d.shape[0]
    moves = ((d, own_d), (fx, own_x), (fy, own_y))

    def copy(k, t):
        return pltpu.make_async_copy(moves[k][0].at[t], moves[k][1].at[t], sems.at[k, t])

    for t in range(steps):
        for k in range(3):
            copy(k, t).start()

    def wait(t):
        for k in range(3):
            copy(k, t).wait()

    prox_cells((own_d, own_x, own_y), (nd, nx, ny), wait)


def forward_body(last_place, place, d, fx, fy, nd, nx, ny, src, edge, ch, cl, out, new_edge, kept, rh, rl):
    fresh = newton(edge[0], edge[1], edge[2])
    for k in range(3):
        new_edge[k] = fresh[k]
    residual_modes(place[0], last_place, d, fx, fy, nd, nx, ny, src, edge[1], fresh[1], ch, cl, out, kept, rh, rl)


def middle_body(last_place, screen, place, y, d, fx, fy, src, edge, kept_sum, ch, cl, nd, nx, ny, out, new_edge, kept, u, rh, rl):
    steps, rows, _ = d.shape
    pairs = steps // 2
    for pair in range(pairs):
        transform_back(y, ch, cl, u, pair, 2 * pairs + 1)
    transform_back(y, ch, cl, u, pairs, 2 * pairs + 1, True)
    at = steps * rows
    u[at + rows : at + rows + TAKEN, :] = u[at + KEPT : at + KEPT + TAKEN, :]
    fill_plane(u, steps, rows, screen, kept_sum[...])
    fresh = newton(*dual_step(d, fx, fy, edge, u, nd, nx, ny))
    for k in range(3):
        new_edge[k] = fresh[k]
    prox_cells((nd, nx, ny), (nd, nx, ny))
    residual_modes(place[0], last_place, d, fx, fy, nd, nx, ny, src, edge[1], fresh[1], ch, cl, out, kept, rh, rl)
    kept[...] = kept[...] + kept_sum[...]


def last_body(y, ch, cl, u, flat, sems):
    steps, rows, _ = u.shape
    copies = []
    for pair in range(steps // 2):
        transform_back(y, ch, cl, flat, pair, steps)
        for t in (2 * pair, 2 * pair + 1):
            copies.append(pltpu.make_async_copy(flat.at[pl.ds(t * rows, rows), :], u.at[t], sems.at[t]))
            copies[-1].start()
    for copy in copies:
        copy.wait()


def solve_body(slabs, places, steps, screen, with_sum, with_edges, *refs):
    if with_sum:
        place, values, z, ch, cl, wh, wl, vh, vl, across, around, so_far, out, total, field = refs
    else:
        place, values, z, ch, cl, wh, wl, vh, vl, across, around, out, total, field = refs
    length = slabs * steps
    pairs = steps // 2
    lanes = z.shape[1]
    rows = lanes // 2
    lane = lax.broadcasted_iota(jnp.int32, (slabs, lanes), 1)
    low_half = lane < rows

    def swap(a, b):
        return jnp.where(low_half, a, pltpu.roll(b, rows, 1)), jnp.where(low_half, pltpu.roll(a, rows, 1), b)

    group = 2 * pairs + 1

    def arrived(place, item):
        return z[pl.ds(place * group + item, slabs, stride=places * group), :]

    for q in range(places // 2):
        span = slice(q * lanes, (q + 1) * lanes)
        planes = swap(arrived(2 * q, 2 * pairs), arrived(2 * q + 1, 2 * pairs))
        for mode in range(2):
            for pair in range(pairs):
                item = mode * pairs + pair
                first, second = swap(arrived(2 * q, item), arrived(2 * q + 1, item))
                if pair == 0:
                    first = first - pltpu.roll(planes[mode], 1, 0)
                top = mode * length + 2 * pair * slabs
                field[top : top + slabs, span] = first
                field[top + slabs : top + 2 * slabs, span] = second
    cosine = (ch[...], cl[...])
    for mode in range(2):
        span = slice(mode * length, (mode + 1) * length)
        field[span, :] = dot3((wh[...], wl[...]), halves(field[span, :]), NN)
    modes = dot3(halves(field[...]), cosine, NT)
    for mode in range(2):
        span = slice(mode * length, (mode + 1) * length)
        solved = modes[span, :] / (around[...] + across[...] + (values[place[1] + mode] + screen))
        if with_sum:
            solved = solved + so_far[span, :]
        total[span, :] = solved
    field[...] = dot3(halves(total[...]), cosine, NN)
    for mode in range(2):
        span = slice(mode * length, (mode + 1) * length)
        field[span, :] = dot3((vh[...], vl[...]), halves(field[span, :]), NN)
    group_out = 2 * pairs + 1 if with_edges else 2 * pairs

    def leaving(place, item):
        return pl.ds(place * group_out + item, slabs, stride=places * group_out)

    for q in range(places // 2):
        span = slice(q * lanes, (q + 1) * lanes)
        for mode in range(2):
            for pair in range(pairs):
                at = mode * length + 2 * pair * slabs
                first, second = swap(field[at : at + slabs, span], field[at + slabs : at + 2 * slabs, span])
                out[leaving(2 * q, mode * pairs + pair), :] = first
                out[leaving(2 * q + 1, mode * pairs + pair), :] = second
        if not with_edges:
            continue
        planes = swap(*[pltpu.roll(field[m * length : m * length + slabs, span], slabs - 1, 0) for m in range(2)])
        for spot, value in zip((2 * q, 2 * q + 1), planes):
            after = (spot + 1) * rows if spot + 1 < places else (spot + 1) * rows - 1
            before = max(spot * rows - 1, 0)
            for mode in range(2):
                top = mode * length
                at = mode * rows + KEPT
                for t in range(steps):
                    column = field[top + t * slabs : top + (t + 1) * slabs, after : after + 1]
                    value = jnp.where(lane == at + t, column, value)
                for t in range(steps + 1):
                    column = field[top + (t % steps) * slabs : top + (t % steps + 1) * slabs, before : before + 1]
                    if t == steps:
                        column = pltpu.roll(jnp.broadcast_to(column, (slabs, lanes)), slabs - 1, 0)
                    value = jnp.where(lane == at + steps + t, column, value)
            out[leaving(spot, 2 * pairs), :] = value


def local(density, flux_x, flux_y, source):
    steps, rows, width = density.shape
    slabs = lax.axis_size("tm")
    places = lax.axis_size("space")
    length = steps * slabs
    screen = SLOW_LOOP / float(length * length)
    order = np.concatenate([np.arange(0, width, 2), np.arange(1, width, 2)])
    ch, cl = (jnp.asarray(m) for m in np_halves(cosine_matrix(width)[order]))
    basis, loop_values = loop_basis(length, slabs)
    wh, wl = (jnp.asarray(m) for m in np_halves(basis))
    vh, vl = (jnp.asarray(m) for m in np_halves(np.ascontiguousarray(basis.T)))
    spectrum = neumann_spectrum(width)
    place = lax.axis_index("space")
    first = 2 * (lax.axis_index("tm") * places + place)
    values = jnp.asarray(spectrum)
    across = jnp.asarray(spectrum[order][None, :])
    around = jnp.asarray(loop_values[:, None])
    place = jnp.stack([place, first]).astype(jnp.int32)
    nbytes = density.size * 4
    mega = density.size * width * 6
    field = (steps, rows, width)
    edge_shape = (3, steps, width)
    lanes = 2 * rows
    devices = slabs * places

    def packed(items):
        return (devices * items, lanes)

    items = steps + 1

    def exchange(value):
        shape = value.shape
        value = value.reshape(devices, 1, shape[0] // devices * lanes)
        value = lax.all_to_all(value, BOTH, split_axis=0, concat_axis=0, tiled=True)
        return value.reshape(shape)

    edge = lax.ppermute(last_rows(density, flux_x, flux_y), "space", [(i, i + 1) for i in range(places - 1)])
    split = [pltpu.VMEM(((steps + 2) * rows, width), bf16)] * 2
    block = (BLOCK, width)
    new_d, new_x, new_y, density, flux_x, flux_y = call(
        prox_body, [field] * 6, scratch=[pltpu.SemaphoreType.DMA((3, steps))], far=3,
        cost=(density.size * 200, 6 * nbytes), name="prox",
    )(*map(stay, (density, flux_x, flux_y)))
    modes, edge, kept = call(
        functools.partial(forward_body, places - 1), [packed(items), edge_shape, block],
        scratch=split, scalars=1, n_in=10, cost=(mega, 8 * nbytes), name="forward",
    )(place, density, flux_x, flux_y, new_d, new_x, new_y, source, edge, ch, cl)
    density, flux_x, flux_y = new_d, new_x, new_y
    total = ()
    for iteration in range(ITERS):
        final = iteration + 1 == ITERS
        modes = exchange(modes)
        modes, solved = call(
            functools.partial(solve_body, slabs, places, steps, screen, bool(total), not final),
            [packed(steps if final else items), (2 * length, width)],
            scratch=[pltpu.VMEM((2 * length, width), f32)],
            scalars=2, n_in=9 + len(total), cost=(3 * mega, 6 * nbytes), name="solve",
        )(place, values, modes, ch, cl, wh, wl, vh, vl, across, around, *total)
        total = (solved,)
        modes = exchange(modes)
        if final:
            break
        density, flux_x, flux_y, modes, edge, kept = call(
            functools.partial(middle_body, places - 1, screen), [field] * 3 + [packed(items), edge_shape, block],
            scratch=[pltpu.VMEM(((steps + 1) * rows + BLOCK, width), f32)] + split,
            scalars=1, n_in=9, cost=(2 * mega, 10 * nbytes), name="middle",
        )(place, modes, density, flux_x, flux_y, source, edge, kept, ch, cl)
    (potential,) = call(
        last_body, [field], scratch=[pltpu.VMEM((steps * rows, width), f32), pltpu.SemaphoreType.DMA((steps,))],
        n_in=3, far_out=True, cost=(mega, 3 * nbytes), name="last",
    )(modes, ch, cl)
    return density, flux_x, flux_y, potential


def solution(mesh):
    spec = P("tm", "space", None)
    return jax.shard_map(local, mesh=mesh, in_specs=(spec,) * 4, out_specs=(spec,) * 4, check_vma=False)
```

```python
import functools

import jax
import jax.numpy as jnp
import numpy as np
from jax import lax
from jax.experimental import pallas as pl
from jax.experimental.pallas import tpu as pltpu
from jax.sharding import PartitionSpec as P

ITERS = 3
NEWTON = 10
TAU_STEP = 1.0
SLOW_LOOP = 2.25
INTERPRET = False
GRANT = 20 << 20
KEPT = 8
TAKEN = 9
BLOCK = 16
BOTH = ("tm", "space")
f32 = jnp.float32
bf16 = jnp.bfloat16
NN = (((1,), (0,)), ((), ()))
NT = (((1,), (1,)), ((), ()))
TN = (((0,), (0,)), ((), ()))


def halves(value):
    high = value.astype(bf16)
    return high, (value - high.astype(f32)).astype(bf16)


def dot3(left, right, dims):
    dot = functools.partial(lax.dot_general, dimension_numbers=dims, preferred_element_type=f32)
    return dot(left[0], right[0]) + (dot(left[0], right[1]) + dot(left[1], right[0]))


def cosine_matrix(points):
    one = np.float32
    frequency = np.arange(points, dtype=one)[:, None]
    sample = np.arange(points, dtype=one)[None, :]
    scaling = np.where(frequency == 0, np.sqrt(one(1.0 / points)), np.sqrt(one(2.0 / points))).astype(one)
    angle = one(np.pi) * (sample + one(0.5)) * frequency / one(points)
    return (scaling * np.cos(angle.astype(np.float64)).astype(one)).astype(one)


def neumann_spectrum(points):
    half_angle = np.pi * np.arange(points) / (2.0 * points)
    return (4.0 * np.sin(half_angle) ** 2).astype(np.float32)


def loop_basis(length, slabs):
    rows = [np.full(length, np.sqrt(1.0 / length))]
    values = [0.0]
    moment = np.arange(length)
    for k in range(1, length // 2):
        angle = 2.0 * np.pi * ((k * moment) % length) / length
        rows += [np.sqrt(2.0 / length) * np.cos(angle), np.sqrt(2.0 / length) * np.sin(angle)]
        values += [4.0 * np.sin(np.pi * k / length) ** 2] * 2
    rows.append(np.sqrt(1.0 / length) * (-1.0) ** moment)
    values.append(4.0)
    basis = np.stack(rows).reshape(length, slabs, length // slabs).transpose(0, 2, 1).reshape(length, length)
    return basis.astype(np.float32), np.asarray(values, np.float32)


def np_halves(matrix):
    high = matrix.astype(bf16)
    return high, (matrix - high.astype(np.float32)).astype(bf16)


def call(body, outs, scratch=(), scalars=0, far=0, n_in=0, far_out=False, cost=None, **kw):
    vmem = pl.BlockSpec(memory_space=pltpu.VMEM)
    smem = pl.BlockSpec(memory_space=pltpu.SMEM)
    hbm = pl.BlockSpec(memory_space=pltpu.HBM)
    return pl.pallas_call(
        body,
        out_shape=[jax.ShapeDtypeStruct(s, f32) if far_out else pltpu.VMEM(s, f32) for s in outs],
        in_specs=[smem] * scalars + [hbm] * far + [vmem] * n_in,
        out_specs=[hbm if far_out else vmem] * len(outs),
        scratch_shapes=list(scratch),
        cost_estimate=pl.CostEstimate(flops=int(cost[0]), bytes_accessed=int(cost[1]), transcendentals=0),
        compiler_params=pltpu.CompilerParams(vmem_limit_bytes=GRANT),
        interpret=INTERPRET,
        **kw,
    )


def newton(mass, along_x, along_y):
    target = 0.5 * TAU_STEP * (along_x * along_x + along_y * along_y)
    root = jnp.maximum(mass, 0.0) + jnp.exp(jnp.log(target) * (1.0 / 3.0))
    shifted = root + TAU_STEP
    half_base = 0.5 * (mass + TAU_STEP)
    quarter = 0.25 * target
    for _ in range(NEWTON):
        half = 0.5 * shifted
        product = shifted * (shifted - half_base)
        shifted = jnp.maximum((half * product + quarter) / (product - half * half), TAU_STEP)
    root = shifted - TAU_STEP
    factor = root / shifted
    return root, factor * along_x, factor * along_y


def prox_cells(source, result, wait=None):
    steps, rows, width = result[0].shape
    chunk = 32
    per = rows // chunk

    def step(index, carry):
        t = index // per
        if wait is not None:
            pl.when(index % per == 0)(lambda: wait(t))
        span = pl.ds(pl.multiple_of((index % per) * chunk, chunk), chunk)
        out = newton(*[ref[t, span, :] for ref in source])
        for ref, value in zip(result, out):
            ref[t, span, :] = value
        return carry

    lax.fori_loop(0, steps * per, step, 0)


def transform_back(y, ch, cl, u, pair, group):
    count = y.shape[0] // group
    lanes = y.shape[1]
    even = y[pl.ds(pair, count, stride=group), :]
    odd = y[pl.ds(group // 2 + pair, count, stride=group), :]
    u[pair * lanes : (pair + 1) * lanes, :] = dot3(halves(jnp.concatenate([even, odd], axis=0)), (ch[...], cl[...]), TN)


def other_step(here, beyond, above, below, screen, residual_sum):
    width = here.shape[1]
    column = lax.broadcasted_iota(jnp.int32, here.shape, 1)
    right = jnp.where(column == width - 1, here, pltpu.roll(here, width - 1, 1))
    left = jnp.where(column == 0, here, pltpu.roll(here, 1, 1))
    value = (here - beyond) + (here - above) + (here - below) + (here - right) + (here - left)
    return here + (value + (screen * here - residual_sum))


def fill_steps(u, steps, rows, screen, kept_sum):
    edge = (steps + 1) * rows
    u[edge : edge + TAKEN, :] = u[KEPT : KEPT + TAKEN, :]
    at = rows + KEPT
    value = other_step(
        u[at : at + BLOCK, :], u[at + rows : at + rows + BLOCK, :], u[at - 1 : at - 1 + BLOCK, :],
        u[at + 1 : at + 1 + BLOCK, :], screen, kept_sum[:BLOCK, :],
    )
    row = lax.broadcasted_iota(jnp.int32, value.shape, 0)
    u[KEPT : KEPT + BLOCK, :] = jnp.where(row < TAKEN, value, u[KEPT : KEPT + BLOCK, :])
    at = (steps - 1) * rows
    here = u[at : at + rows, :]
    row = lax.broadcasted_iota(jnp.int32, here.shape, 0)
    above = jnp.where(row == 0, u[edge + 2 * steps - 1 : edge + 2 * steps, :], pltpu.roll(here, 1, 0))
    below = jnp.where(row == rows - 1, u[edge + steps - 1 : edge + steps, :], pltpu.roll(here, rows - 1, 0))
    value = other_step(here, u[at - rows : at, :], above, below, screen, kept_sum[BLOCK:, :])
    u[at + rows : at + 2 * rows, :] = value


def dual_step(d, fx, fy, edge, u, nd, nx, ny):
    steps, rows, width = d.shape
    below_at = (steps + 1) * rows
    above_at = below_at + steps
    end_row = lax.broadcasted_iota(jnp.int32, (rows, width), 0) == rows - 1
    end_column = lax.broadcasted_iota(jnp.int32, (rows, width), 1) == width - 1
    for t in range(steps):
        here = u[t * rows : (t + 1) * rows, :]
        later = u[(t + 1) * rows : (t + 2) * rows, :]
        below = jnp.where(end_row, u[below_at + t : below_at + t + 1, :], pltpu.roll(here, rows - 1, 0))
        right = jnp.where(end_column, here, pltpu.roll(here, width - 1, 1))
        nd[t] = d[t] - TAU_STEP * (here - later)
        nx[t] = fx[t] - TAU_STEP * (here - below)
        ny[t] = fy[t] - TAU_STEP * (here - right)
    here = u[above_at : above_at + steps, :]
    later = u[above_at + 1 : above_at + 1 + steps, :]
    below = jnp.concatenate([u[t * rows : t * rows + 1, :] for t in range(steps)], axis=0)
    right = jnp.where(end_column[:steps, :], here, pltpu.roll(here, width - 1, 1))
    return (
        edge[0] - TAU_STEP * (here - later),
        edge[1] - TAU_STEP * (here - below),
        edge[2] - TAU_STEP * (here - right),
    )


def residual_modes(place, last_place, d, fx, fy, nd, nx, ny, src, edge_x, new_edge_x, ch, cl, out, kept, rh, rl):
    steps, rows, width = d.shape
    shape = (rows, width)
    row = lax.broadcasted_iota(jnp.int32, shape, 0)
    column = lax.broadcasted_iota(jnp.int32, shape, 1)
    final_row = (row == rows - 1) & (place == last_place)
    edge_bar = jnp.where(place == 0, 0.0, 2.0 * new_edge_x - edge_x)
    before = None
    for t in range(steps):
        mass = 2.0 * nd[t] - d[t]
        along_x = 2.0 * nx[t] - fx[t]
        along_y = 2.0 * ny[t] - fy[t]
        x_before = jnp.where(row == 0, edge_bar[t : t + 1, :], pltpu.roll(along_x, 1, 0))
        y_before = jnp.where(column == 0, 0.0, pltpu.roll(along_y, 1, 1))
        value = mass if before is None else mass - before
        value = value + (jnp.where(final_row, 0.0, along_x) - x_before)
        value = value + (jnp.where(column == width - 1, 0.0, along_y) - y_before)
        value = value - src[t]
        before = mass
        high, low = halves(value)
        rh[t * rows : (t + 1) * rows, :] = high
        rl[t * rows : (t + 1) * rows, :] = low
        if t == 1:
            kept[:BLOCK, :] = value[KEPT : KEPT + BLOCK, :]
        if t == steps - 1:
            kept[BLOCK:, :] = value
    high, low = halves(before)
    for t in (steps, steps + 1):
        rh[t * rows : (t + 1) * rows, :] = high
        rl[t * rows : (t + 1) * rows, :] = low
    modes = dot3((ch[...], cl[...]), (rh[...], rl[...]), NT)
    lanes = 2 * rows
    pairs = steps // 2
    count = width // 2
    group = 2 * pairs + 1
    for pair in range(pairs):
        span = slice(pair * lanes, (pair + 1) * lanes)
        out[pl.ds(pair, count, stride=group), :] = modes[:count, span]
        out[pl.ds(pairs + pair, count, stride=group), :] = modes[count:, span]
    span = slice(pairs * lanes, (pairs + 1) * lanes)
    low_half = lax.broadcasted_iota(jnp.int32, (count, lanes), 1) < rows
    out[pl.ds(2 * pairs, count, stride=group), :] = jnp.where(low_half, modes[:count, span], modes[count:, span])


def edge_body(d, fx, fy, edge):
    rows = d.shape[1]
    for k, ref in enumerate((d, fx, fy)):
        for t in range(d.shape[0]):
            edge[k, t : t + 1, :] = ref[t, rows - 1 :, :]


def stay(value):
    return value if INTERPRET else pltpu.with_memory_space_constraint(value, pltpu.HBM)


def last_rows(density, flux_x, flux_y):
    steps, rows, width = density.shape
    block = pl.BlockSpec((steps, 8, width), lambda i: (0, rows // 8 - 1, 0))
    return pl.pallas_call(
        edge_body,
        grid=(1,),
        out_shape=jax.ShapeDtypeStruct((3, steps, width), f32),
        in_specs=[block] * 3,
        out_specs=pl.BlockSpec((3, steps, width), lambda i: (0, 0, 0)),
        compiler_params=pltpu.CompilerParams(vmem_limit_bytes=GRANT),
        interpret=INTERPRET,
        name="edges",
    )(*map(stay, (density, flux_x, flux_y)))


def prox_body(d, fx, fy, nd, nx, ny, own_d, own_x, own_y, sems):
    steps = d.shape[0]
    moves = ((d, own_d), (fx, own_x), (fy, own_y))

    def copy(k, t):
        return pltpu.make_async_copy(moves[k][0].at[t], moves[k][1].at[t], sems.at[k, t])

    for t in range(steps):
        for k in range(3):
            copy(k, t).start()

    def wait(t):
        for k in range(3):
            copy(k, t).wait()

    prox_cells((own_d, own_x, own_y), (nd, nx, ny), wait)


def forward_body(last_place, place, d, fx, fy, nd, nx, ny, src, edge, ch, cl, out, new_edge, kept, rh, rl):
    fresh = newton(edge[0], edge[1], edge[2])
    for k in range(3):
        new_edge[k] = fresh[k]
    residual_modes(place[0], last_place, d, fx, fy, nd, nx, ny, src, edge[1], fresh[1], ch, cl, out, kept, rh, rl)


def middle_body(last_place, screen, place, y, d, fx, fy, src, edge, kept_sum, ch, cl, nd, nx, ny, out, new_edge, kept, u, rh, rl):
    steps, rows, _ = d.shape
    for pair in range(steps // 2):
        transform_back(y, ch, cl, u, pair, steps)
    fill_steps(u, steps, rows, screen, kept_sum)
    fresh = newton(*dual_step(d, fx, fy, edge, u, nd, nx, ny))
    for k in range(3):
        new_edge[k] = fresh[k]
    prox_cells((nd, nx, ny), (nd, nx, ny))
    residual_modes(place[0], last_place, d, fx, fy, nd, nx, ny, src, edge[1], fresh[1], ch, cl, out, kept, rh, rl)
    kept[...] = kept[...] + kept_sum[...]


def last_body(y, ch, cl, u, flat, sems):
    steps, rows, _ = u.shape
    copies = []
    for pair in range(steps // 2):
        transform_back(y, ch, cl, flat, pair, steps)
        for t in (2 * pair, 2 * pair + 1):
            copies.append(pltpu.make_async_copy(flat.at[pl.ds(t * rows, rows), :], u.at[t], sems.at[t]))
            copies[-1].start()
    for copy in copies:
        copy.wait()


def solve_body(slabs, places, steps, screen, with_sum, with_edges, *refs):
    if with_sum:
        z, ch, cl, wh, wl, vh, vl, inverse, so_far, out, total, field = refs
    else:
        place, values, z, ch, cl, wh, wl, vh, vl, across, around, out, total, inverse, field = refs
        for mode in range(2):
            inverse[mode * slabs * steps : (mode + 1) * slabs * steps, :] = 1.0 / (
                around[...] + across[...] + (values[place[1] + mode] + screen)
            )
    length = slabs * steps
    pairs = steps // 2
    lanes = z.shape[1]
    rows = lanes // 2
    lane = lax.broadcasted_iota(jnp.int32, (slabs, lanes), 1)
    low_half = lane < rows

    def swap(a, b):
        return jnp.where(low_half, a, pltpu.roll(b, rows, 1)), jnp.where(low_half, pltpu.roll(a, rows, 1), b)

    group = 2 * pairs + 1

    def arrived(place, item):
        return z[pl.ds(place * group + item, slabs, stride=places * group), :]

    for q in range(places // 2):
        span = slice(q * lanes, (q + 1) * lanes)
        planes = swap(arrived(2 * q, 2 * pairs), arrived(2 * q + 1, 2 * pairs))
        for mode in range(2):
            for pair in range(pairs):
                item = mode * pairs + pair
                first, second = swap(arrived(2 * q, item), arrived(2 * q + 1, item))
                if pair == 0:
                    first = first - pltpu.roll(planes[mode], 1, 0)
                top = mode * length + 2 * pair * slabs
                field[top : top + slabs, span] = first
                field[top + slabs : top + 2 * slabs, span] = second
    cosine = (ch[...], cl[...])
    for mode in range(2):
        span = slice(mode * length, (mode + 1) * length)
        field[span, :] = dot3((wh[...], wl[...]), halves(field[span, :]), NN)
    solved = dot3(halves(field[...]), cosine, NT) * inverse[...]
    if with_sum:
        solved = solved + so_far[...]
    total[...] = solved
    field[...] = dot3(halves(solved), cosine, NN)
    for mode in range(2):
        span = slice(mode * length, (mode + 1) * length)
        field[span, :] = dot3((vh[...], vl[...]), halves(field[span, :]), NN)
    def leaving(place, item):
        return pl.ds(place * steps + item, slabs, stride=places * steps)

    def with_row_values(value, top, spot):
        after = (spot + 1) * rows if spot + 1 < places else (spot + 1) * rows - 1
        before = max(spot * rows - 1, 0)
        for t in range(steps):
            column = field[top + t * slabs : top + (t + 1) * slabs, after : after + 1]
            value = jnp.where(lane == KEPT + t, column, value)
        for t in range(steps + 1):
            column = field[top + (t % steps) * slabs : top + (t % steps + 1) * slabs, before : before + 1]
            if t == steps:
                column = pltpu.roll(jnp.broadcast_to(column, (slabs, lanes)), slabs - 1, 0)
            value = jnp.where(lane == KEPT + steps + t, column, value)
        return value

    for q in range(places // 2):
        span = slice(q * lanes, (q + 1) * lanes)
        for mode in range(2):
            for pair in range(pairs):
                at = mode * length + 2 * pair * slabs
                both = swap(field[at : at + slabs, span], field[at + slabs : at + 2 * slabs, span])
                for spot, value in zip((2 * q, 2 * q + 1), both):
                    if with_edges and pair == 0:
                        value = with_row_values(value, mode * length, spot)
                    out[leaving(spot, mode * pairs + pair), :] = value


def local(density, flux_x, flux_y, source):
    steps, rows, width = density.shape
    slabs = lax.axis_size("tm")
    places = lax.axis_size("space")
    length = steps * slabs
    screen = SLOW_LOOP / float(length * length)
    order = np.concatenate([np.arange(0, width, 2), np.arange(1, width, 2)])
    ch, cl = (jnp.asarray(m) for m in np_halves(cosine_matrix(width)[order]))
    basis, loop_values = loop_basis(length, slabs)
    wh, wl = (jnp.asarray(m) for m in np_halves(basis))
    vh, vl = (jnp.asarray(m) for m in np_halves(np.ascontiguousarray(basis.T)))
    spectrum = neumann_spectrum(width)
    place = lax.axis_index("space")
    first = 2 * (lax.axis_index("tm") * places + place)
    values = jnp.asarray(spectrum)
    across = jnp.asarray(spectrum[order][None, :])
    around = jnp.asarray(loop_values[:, None])
    place = jnp.stack([place, first]).astype(jnp.int32)
    nbytes = density.size * 4
    mega = density.size * width * 6
    field = (steps, rows, width)
    edge_shape = (3, steps, width)
    lanes = 2 * rows
    devices = slabs * places

    def packed(items):
        return (devices * items, lanes)

    items = steps + 1

    def exchange(value):
        shape = value.shape
        value = value.reshape(devices, 1, shape[0] // devices * lanes)
        value = lax.all_to_all(value, BOTH, split_axis=0, concat_axis=0, tiled=True)
        return value.reshape(shape)

    edge = lax.ppermute(last_rows(density, flux_x, flux_y), "space", [(i, i + 1) for i in range(places - 1)])
    split = [pltpu.VMEM(((steps + 2) * rows, width), bf16)] * 2
    block = (BLOCK + rows, width)
    square = (2 * length, width)
    new_d, new_x, new_y, density, flux_x, flux_y = call(
        prox_body, [field] * 6, scratch=[pltpu.SemaphoreType.DMA((3, steps))], far=3,
        cost=(density.size * 200, 6 * nbytes), name="prox",
    )(*map(stay, (density, flux_x, flux_y)))
    modes, edge, kept = call(
        functools.partial(forward_body, places - 1), [packed(items), edge_shape, block],
        scratch=split, scalars=1, n_in=10, cost=(mega, 8 * nbytes), name="forward",
    )(place, density, flux_x, flux_y, new_d, new_x, new_y, source, edge, ch, cl)
    density, flux_x, flux_y = new_d, new_x, new_y
    for iteration in range(ITERS):
        final = iteration + 1 == ITERS
        modes = exchange(modes)
        body = functools.partial(solve_body, slabs, places, steps, screen, iteration > 0, not final)
        settings = dict(scratch=[pltpu.VMEM(square, f32)], n_in=9, cost=(3 * mega, 6 * nbytes), name="solve")
        shapes = [packed(steps), square]
        matrices = (ch, cl, wh, wl, vh, vl)
        if iteration:
            modes, total = call(body, shapes, **settings)(modes, *matrices, inverse, total)
        else:
            modes, total, inverse = call(body, shapes + [square], scalars=2, **settings)(
                place, values, modes, *matrices, across, around
            )
        modes = exchange(modes)
        if final:
            break
        density, flux_x, flux_y, modes, edge, kept = call(
            functools.partial(middle_body, places - 1, screen), [field] * 3 + [packed(items), edge_shape, block],
            scratch=[pltpu.VMEM(((steps + 1) * rows + BLOCK, width), f32)] + split,
            scalars=1, n_in=9, cost=(2 * mega, 10 * nbytes), name="middle",
        )(place, modes, density, flux_x, flux_y, source, edge, kept, ch, cl)
    (potential,) = call(
        last_body, [field], scratch=[pltpu.VMEM((steps * rows, width), f32), pltpu.SemaphoreType.DMA((steps,))],
        n_in=3, far_out=True, cost=(mega, 3 * nbytes), name="last",
    )(modes, ch, cl)
    return density, flux_x, flux_y, potential


def solution(mesh):
    spec = P("tm", "space", None)
    return jax.shard_map(local, mesh=mesh, in_specs=(spec,) * 4, out_specs=(spec,) * 4, check_vma=False)
```

```python
import functools

import jax
import jax.numpy as jnp
import numpy as np
from jax import lax
from jax.experimental import pallas as pl
from jax.experimental.pallas import tpu as pltpu
from jax.sharding import PartitionSpec as P

ITERS = 3
NEWTON = 10
TAU_STEP = 1.0
SLOW_LOOP = 2.25
INTERPRET = False
GRANT = 20 << 20
KEPT = 8
TAKEN = 13
BLOCK = 16
ORDER = (1, 2, 0, 3)
BOTH = ("tm", "space")
f32 = jnp.float32
bf16 = jnp.bfloat16
NN = (((1,), (0,)), ((), ()))
NT = (((1,), (1,)), ((), ()))
TN = (((0,), (0,)), ((), ()))


def halves(value):
    high = value.astype(bf16)
    return high, (value - high.astype(f32)).astype(bf16)


def dot3(left, right, dims):
    dot = functools.partial(lax.dot_general, dimension_numbers=dims, preferred_element_type=f32)
    return dot(left[0], right[0]) + (dot(left[0], right[1]) + dot(left[1], right[0]))


def cosine_matrix(points):
    one = np.float32
    frequency = np.arange(points, dtype=one)[:, None]
    sample = np.arange(points, dtype=one)[None, :]
    scaling = np.where(frequency == 0, np.sqrt(one(1.0 / points)), np.sqrt(one(2.0 / points))).astype(one)
    angle = one(np.pi) * (sample + one(0.5)) * frequency / one(points)
    return (scaling * np.cos(angle.astype(np.float64)).astype(one)).astype(one)


def neumann_spectrum(points):
    half_angle = np.pi * np.arange(points) / (2.0 * points)
    return (4.0 * np.sin(half_angle) ** 2).astype(np.float32)


def loop_basis(length, slabs):
    rows = [np.full(length, np.sqrt(1.0 / length))]
    values = [0.0]
    moment = np.arange(length)
    for k in range(1, length // 2):
        angle = 2.0 * np.pi * ((k * moment) % length) / length
        rows += [np.sqrt(2.0 / length) * np.cos(angle), np.sqrt(2.0 / length) * np.sin(angle)]
        values += [4.0 * np.sin(np.pi * k / length) ** 2] * 2
    rows.append(np.sqrt(1.0 / length) * (-1.0) ** moment)
    values.append(4.0)
    basis = np.stack(rows).reshape(length, slabs, length // slabs).transpose(0, 2, 1).reshape(length, length)
    return basis.astype(np.float32), np.asarray(values, np.float32)


def np_halves(matrix):
    high = matrix.astype(bf16)
    return high, (matrix - high.astype(np.float32)).astype(bf16)


def call(body, outs, scratch=(), scalars=0, far=0, n_in=0, far_out=False, cost=None, **kw):
    vmem = pl.BlockSpec(memory_space=pltpu.VMEM)
    smem = pl.BlockSpec(memory_space=pltpu.SMEM)
    hbm = pl.BlockSpec(memory_space=pltpu.HBM)
    return pl.pallas_call(
        body,
        out_shape=[jax.ShapeDtypeStruct(s, f32) if far_out else pltpu.VMEM(s, f32) for s in outs],
        in_specs=[smem] * scalars + [hbm] * far + [vmem] * n_in,
        out_specs=[hbm if far_out else vmem] * len(outs),
        scratch_shapes=list(scratch),
        cost_estimate=pl.CostEstimate(flops=int(cost[0]), bytes_accessed=int(cost[1]), transcendentals=0),
        compiler_params=pltpu.CompilerParams(vmem_limit_bytes=GRANT),
        interpret=INTERPRET,
        **kw,
    )


def newton(mass, along_x, along_y):
    target = 0.5 * TAU_STEP * (along_x * along_x + along_y * along_y)
    root = jnp.maximum(mass, 0.0) + jnp.exp(jnp.log(target) * (1.0 / 3.0))
    shifted = root + TAU_STEP
    half_base = 0.5 * (mass + TAU_STEP)
    quarter = 0.25 * target
    for _ in range(NEWTON):
        half = 0.5 * shifted
        product = shifted * (shifted - half_base)
        shifted = jnp.maximum((half * product + quarter) / (product - half * half), TAU_STEP)
    root = shifted - TAU_STEP
    factor = root / shifted
    return root, factor * along_x, factor * along_y


def prox_cells(source, result, wait=None):
    steps, rows, width = result[0].shape
    chunk = 16
    per = rows // chunk

    def step(index, carry):
        t = index // per
        if wait is not None:
            pl.when(index % per == 0)(lambda: wait(t))
        span = pl.ds(pl.multiple_of((index % per) * chunk, chunk), chunk)
        out = newton(*[ref[t, span, :] for ref in source])
        for ref, value in zip(result, out):
            ref[t, span, :] = value
        return carry

    lax.fori_loop(0, steps * per, step, 0)


def send_values(y, hat_sum, qh, ql, pick, scale):
    count = y.shape[0] // 3
    lanes = y.shape[1]
    both = y[pl.ds(2, count, stride=3), :]
    outer = jnp.concatenate([y[pl.ds(0, count, stride=3), :], y[pl.ds(1, count, stride=3), :]], axis=0)
    edge = jnp.concatenate([both, pltpu.roll(both, lanes // 2, 1)], axis=0)
    sine = (qh[...], ql[...])
    high, low = (lax.dot_general(part, pick[...], NN, preferred_element_type=f32) for part in halves(edge))
    moved = high + low
    modes = dot3(halves(outer + hat_sum[...] + moved[:, lanes:]), sine, NN)
    inner = dot3(halves(modes * scale[...]), sine, NN) + moved[:, :lanes]
    return outer, inner, edge


def fill_slab(u, rows, outer, inner, edge, ch, cl):
    cosine = (ch[...], cl[...])
    value = dot3(halves(outer), cosine, TN)
    u[:rows, :] = value[:rows, :]
    u[3 * rows : 4 * rows, :] = value[rows:, :]
    u[rows : 3 * rows, :] = dot3(halves(inner), cosine, TN)
    if edge is not None:
        u[4 * rows : 5 * rows, :] = dot3(halves(edge), cosine, TN)[:rows, :]


def fill_plane(u, steps, rows, screen, residual_sum):
    at = (steps - 1) * rows + KEPT
    here = u[at : at + BLOCK, :]
    width = here.shape[1]
    column = lax.broadcasted_iota(jnp.int32, here.shape, 1)
    right = jnp.where(column == width - 1, here, pltpu.roll(here, width - 1, 1))
    left = jnp.where(column == 0, here, pltpu.roll(here, 1, 1))
    earlier = u[at - rows : at - rows + BLOCK, :]
    value = (here - earlier) + (here - u[at - 1 : at - 1 + BLOCK, :]) + (here - u[at + 1 : at + 1 + BLOCK, :])
    value = here + (value + (here - right) + (here - left) + screen * here - residual_sum)
    at = steps * rows + KEPT
    row = lax.broadcasted_iota(jnp.int32, here.shape, 0)
    u[at : at + BLOCK, :] = jnp.where(row < TAKEN, value, u[at : at + BLOCK, :])


def dual_step(d, fx, fy, edge, u, nd, nx, ny):
    steps, rows, width = d.shape
    below_at = (steps + 1) * rows
    above_at = below_at + steps
    end_row = lax.broadcasted_iota(jnp.int32, (rows, width), 0) == rows - 1
    end_column = lax.broadcasted_iota(jnp.int32, (rows, width), 1) == width - 1
    for t in range(steps):
        here = u[t * rows : (t + 1) * rows, :]
        later = u[(t + 1) * rows : (t + 2) * rows, :]
        below = jnp.where(end_row, u[below_at + t : below_at + t + 1, :], pltpu.roll(here, rows - 1, 0))
        right = jnp.where(end_column, here, pltpu.roll(here, width - 1, 1))
        nd[t] = d[t] - TAU_STEP * (here - later)
        nx[t] = fx[t] - TAU_STEP * (here - below)
        ny[t] = fy[t] - TAU_STEP * (here - right)
    here = u[above_at : above_at + steps, :]
    later = u[above_at + 1 : above_at + 1 + steps, :]
    below = jnp.concatenate([u[t * rows : t * rows + 1, :] for t in range(steps)], axis=0)
    right = jnp.where(end_column[:steps, :], here, pltpu.roll(here, width - 1, 1))
    return (
        edge[0] - TAU_STEP * (here - later),
        edge[1] - TAU_STEP * (here - below),
        edge[2] - TAU_STEP * (here - right),
    )


def residual_modes(place, last_place, d, fx, fy, nd, nx, ny, src, edge_x, new_edge_x, ch, cl, out, kept, hat, rh, rl):
    steps, rows, width = d.shape
    shape = (rows, width)
    row = lax.broadcasted_iota(jnp.int32, shape, 0)
    column = lax.broadcasted_iota(jnp.int32, shape, 1)
    final_row = (row == rows - 1) & (place == last_place)
    edge_bar = jnp.where(place == 0, 0.0, 2.0 * new_edge_x - edge_x)
    before = None
    for t in range(steps):
        mass = 2.0 * nd[t] - d[t]
        along_x = 2.0 * nx[t] - fx[t]
        along_y = 2.0 * ny[t] - fy[t]
        x_before = jnp.where(row == 0, edge_bar[t : t + 1, :], pltpu.roll(along_x, 1, 0))
        y_before = jnp.where(column == 0, 0.0, pltpu.roll(along_y, 1, 1))
        value = mass if before is None else mass - before
        value = value + (jnp.where(final_row, 0.0, along_x) - x_before)
        value = value + (jnp.where(column == width - 1, 0.0, along_y) - y_before)
        value = value - src[t]
        before = mass
        high, low = halves(value)
        at = ORDER.index(t) * rows
        rh[at : at + rows, :] = high
        rl[at : at + rows, :] = low
    kept[...] = value[KEPT : KEPT + BLOCK, :]
    high, low = halves(before)
    for t in (steps, steps + 1):
        rh[t * rows : (t + 1) * rows, :] = high
        rl[t * rows : (t + 1) * rows, :] = low
    modes = dot3((ch[...], cl[...]), (rh[...], rl[...]), NT)
    lanes = 2 * rows
    hat[...] = modes[:, :lanes]
    pairs = steps // 2
    count = width // 2
    group = 2 * pairs + 1
    for pair in range(pairs):
        span = slice(pair * lanes, (pair + 1) * lanes)
        out[pl.ds(pair, count, stride=group), :] = modes[:count, span]
        out[pl.ds(pairs + pair, count, stride=group), :] = modes[count:, span]
    span = slice(pairs * lanes, (pairs + 1) * lanes)
    low_half = lax.broadcasted_iota(jnp.int32, (count, lanes), 1) < rows
    out[pl.ds(2 * pairs, count, stride=group), :] = jnp.where(low_half, modes[:count, span], modes[count:, span])


def edge_body(d, fx, fy, edge):
    rows = d.shape[1]
    for k, ref in enumerate((d, fx, fy)):
        for t in range(d.shape[0]):
            edge[k, t : t + 1, :] = ref[t, rows - 1 :, :]


def stay(value):
    return value if INTERPRET else pltpu.with_memory_space_constraint(value, pltpu.HBM)


def last_rows(density, flux_x, flux_y):
    steps, rows, width = density.shape
    block = pl.BlockSpec((steps, 8, width), lambda i: (0, rows // 8 - 1, 0))
    return pl.pallas_call(
        edge_body,
        grid=(1,),
        out_shape=jax.ShapeDtypeStruct((3, steps, width), f32),
        in_specs=[block] * 3,
        out_specs=pl.BlockSpec((3, steps, width), lambda i: (0, 0, 0)),
        compiler_params=pltpu.CompilerParams(vmem_limit_bytes=GRANT),
        interpret=INTERPRET,
        name="edges",
    )(*map(stay, (density, flux_x, flux_y)))


def prox_body(d, fx, fy, across, along, nd, nx, ny, own_d, own_x, own_y, scale, sems):
    steps = d.shape[0]
    moves = ((d, own_d), (fx, own_x), (fy, own_y))

    def copy(k, t):
        return pltpu.make_async_copy(moves[k][0].at[t], moves[k][1].at[t], sems.at[k, t])

    for t in range(steps):
        for k in range(3):
            copy(k, t).start()

    scale[...] = 1.0 / (jnp.broadcast_to(across[...], scale.shape[::-1]).T + along[...])

    def wait(t):
        for k in range(3):
            copy(k, t).wait()

    prox_cells((own_d, own_x, own_y), (nd, nx, ny), wait)


def forward_body(last_place, place, d, fx, fy, nd, nx, ny, src, edge, ch, cl, out, new_edge, kept, hat, rh, rl):
    fresh = newton(edge[0], edge[1], edge[2])
    for k in range(3):
        new_edge[k] = fresh[k]
    residual_modes(place[0], last_place, d, fx, fy, nd, nx, ny, src, edge[1], fresh[1], ch, cl, out, kept, hat, rh, rl)


def middle_body(
    last_place, screen, place, y, d, fx, fy, src, edge, kept_sum, hat_sum, ch, cl, qh, ql, pick, scale,
    nd, nx, ny, out, new_edge, kept, hat, u, rh, rl,
):
    steps, rows, _ = d.shape
    fill_slab(u, rows, *send_values(y, hat_sum, qh, ql, pick, scale), ch, cl)
    at = steps * rows
    u[at + rows : at + rows + TAKEN, :] = u[at + KEPT : at + KEPT + TAKEN, :]
    fill_plane(u, steps, rows, screen, kept_sum[...])
    fresh = newton(*dual_step(d, fx, fy, edge, u, nd, nx, ny))
    for k in range(3):
        new_edge[k] = fresh[k]
    prox_cells((nd, nx, ny), (nd, nx, ny))
    residual_modes(place[0], last_place, d, fx, fy, nd, nx, ny, src, edge[1], fresh[1], ch, cl, out, kept, hat, rh, rl)
    kept[...] = kept[...] + kept_sum[...]
    hat[...] = hat[...] + hat_sum[...]


def last_body(y, hat_sum, ch, cl, qh, ql, pick, scale, u, flat, sems):
    steps, rows, _ = u.shape
    outer, inner, _ = send_values(y, hat_sum, qh, ql, pick, scale)
    fill_slab(flat, rows, outer, inner, None, ch, cl)
    copies = [pltpu.make_async_copy(flat.at[pl.ds(t * rows, rows), :], u.at[t], sems.at[t]) for t in range(steps)]
    for copy in copies:
        copy.start()
    for copy in copies:
        copy.wait()


def solve_body(slabs, places, steps, screen, with_sum, *refs):
    if with_sum:
        z, ch, cl, wh, wl, inverse, so_far, out, total, field = refs
    else:
        place, values, z, ch, cl, wh, wl, across, around, out, total, inverse, field = refs
        turned = jnp.broadcast_to(around[...], across.shape[1:] + around.shape[1:]).T
        for mode in range(2):
            inverse[mode * slabs * steps : (mode + 1) * slabs * steps, :] = 1.0 / (
                turned + across[...] + (values[place[1] + mode] + screen)
            )
    length = slabs * steps
    pairs = steps // 2
    lanes = z.shape[1]
    rows = lanes // 2
    lane = lax.broadcasted_iota(jnp.int32, (slabs, lanes), 1)
    low_half = lane < rows

    def swap(a, b):
        return jnp.where(low_half, a, pltpu.roll(b, rows, 1)), jnp.where(low_half, pltpu.roll(a, rows, 1), b)

    group = 2 * pairs + 1

    def arrived(place, item):
        return z[pl.ds(place * group + item, slabs, stride=places * group), :]

    for q in range(places // 2):
        span = slice(q * lanes, (q + 1) * lanes)
        planes = swap(arrived(2 * q, 2 * pairs), arrived(2 * q + 1, 2 * pairs))
        for mode in range(2):
            for pair in range(pairs):
                item = mode * pairs + pair
                first, second = swap(arrived(2 * q, item), arrived(2 * q + 1, item))
                for t, value in zip(ORDER[2 * pair : 2 * pair + 2], (first, second)):
                    if t == 0:
                        value = value - pltpu.roll(planes[mode], 1, 0)
                    top = mode * length + t * slabs
                    field[top : top + slabs, span] = value
    cosine = (ch[...], cl[...])
    for mode in range(2):
        span = slice(mode * length, (mode + 1) * length)
        field[span, :] = dot3((wh[...], wl[...]), halves(field[span, :]), NN)
    solved = dot3(halves(field[...]), cosine, NT) * inverse[...]
    if with_sum:
        solved = solved + so_far[...]
    total[...] = solved
    field[...] = dot3(halves(solved), cosine, NN)
    for mode in range(2):
        span = slice(mode * length, (mode + 1) * length)
        field[span, :] = dot3((wh[...], wl[...]), halves(field[span, :]), TN)
    group_out = 3

    def leaving(place, item):
        return pl.ds(place * group_out + item, slabs, stride=places * group_out)

    for q in range(places // 2):
        span = slice(q * lanes, (q + 1) * lanes)
        for mode in range(2):
            at = mode * length
            end = at + (steps - 1) * slabs
            first, second = swap(field[at : at + slabs, span], field[end : end + slabs, span])
            out[leaving(2 * q, mode), :] = first
            out[leaving(2 * q + 1, mode), :] = second
        planes = swap(*[pltpu.roll(field[m * length : m * length + slabs, span], slabs - 1, 0) for m in range(2)])
        for spot, value in zip((2 * q, 2 * q + 1), planes):
            after = (spot + 1) * rows if spot + 1 < places else (spot + 1) * rows - 1
            before = max(spot * rows - 1, 0)
            for mode in range(2):
                top = mode * length
                at = mode * rows + KEPT
                for t in range(steps):
                    column = field[top + t * slabs : top + (t + 1) * slabs, after : after + 1]
                    value = jnp.where(lane == at + t, column, value)
                for t in range(steps + 1):
                    column = field[top + (t % steps) * slabs : top + (t % steps + 1) * slabs, before : before + 1]
                    if t == steps:
                        column = pltpu.roll(jnp.broadcast_to(column, (slabs, lanes)), slabs - 1, 0)
                    value = jnp.where(lane == at + steps + t, column, value)
                for k, (t, line) in enumerate(((1, 0), (1, rows - 1), (2, 0), (2, rows - 1))):
                    line = spot * rows + line
                    column = field[top + t * slabs : top + (t + 1) * slabs, line : line + 1]
                    value = jnp.where(lane == at + 2 * steps + 1 + k, column, value)
            out[leaving(spot, 2), :] = value


def local(density, flux_x, flux_y, source):
    steps, rows, width = density.shape
    slabs = lax.axis_size("tm")
    places = lax.axis_size("space")
    length = steps * slabs
    screen = SLOW_LOOP / float(length * length)
    order = np.concatenate([np.arange(0, width, 2), np.arange(1, width, 2)])
    ch, cl = (jnp.asarray(m) for m in np_halves(cosine_matrix(width)[order]))
    basis, loop_values = loop_basis(length, slabs)
    wh, wl = (jnp.asarray(m) for m in np_halves(basis))
    spectrum = neumann_spectrum(width)
    place = lax.axis_index("space")
    first = 2 * (lax.axis_index("tm") * places + place)
    values = jnp.asarray(spectrum)
    count = np.arange(rows)
    gaps = rows - 1
    sine = np.sqrt(2.0 / gaps) * np.sin(np.pi * (np.outer(count, count) % (2 * gaps)) / gaps)
    sine[0] = sine[-1] = sine[:, 0] = sine[:, -1] = 0.0
    lines = np.sqrt(0.5) * np.block([[sine, sine], [sine, -sine]])
    lanes_of = 2 * rows
    pick = np.zeros((lanes_of, 2 * lanes_of), np.float32)
    for spot, place_of, line in ((0, 0, 1), (1, rows - 1, rows - 2), (2, rows, rows + 1), (3, 2 * rows - 1, 2 * rows - 2)):
        pick[KEPT + 2 * steps + 1 + spot, (place_of, lanes_of + line)] = 1.0
    inner = [jnp.asarray(m) for m in np_halves(lines.astype(np.float32))]
    inner.append(jnp.asarray(pick.astype(bf16)))
    stiffness = 2.0 - 2.0 * np.cos(np.pi * count / gaps)
    along = jnp.asarray((np.concatenate([1.0 + stiffness, 3.0 + stiffness]) + screen).astype(np.float32)[None, :])
    across = jnp.asarray(spectrum[order][None, :])
    around = jnp.asarray(loop_values[None, :])
    place = jnp.stack([place, first]).astype(jnp.int32)
    nbytes = density.size * 4
    mega = density.size * width * 6
    field = (steps, rows, width)
    edge_shape = (3, steps, width)
    lanes = 2 * rows
    devices = slabs * places

    def packed(items):
        return (devices * items, lanes)

    items = steps + 1

    def exchange(value):
        shape = value.shape
        value = value.reshape(devices, 1, shape[0] // devices * lanes)
        value = lax.all_to_all(value, BOTH, split_axis=0, concat_axis=0, tiled=True)
        return value.reshape(shape)

    edge = lax.ppermute(last_rows(density, flux_x, flux_y), "space", [(i, i + 1) for i in range(places - 1)])
    split = [pltpu.VMEM(((steps + 2) * rows, width), bf16)] * 2
    block = (BLOCK, width)
    square = (2 * length, width)
    hat_shape = (width, lanes)
    new_d, new_x, new_y, density, flux_x, flux_y, scale = call(
        prox_body, [field] * 6 + [hat_shape], scratch=[pltpu.SemaphoreType.DMA((3, steps))], far=3, n_in=2,
        cost=(density.size * 200, 6 * nbytes), name="prox",
    )(*map(stay, (density, flux_x, flux_y)), across, along)
    modes, edge, kept, hat = call(
        functools.partial(forward_body, places - 1), [packed(items), edge_shape, block, hat_shape],
        scratch=split, scalars=1, n_in=10, cost=(mega, 8 * nbytes), name="forward",
    )(place, density, flux_x, flux_y, new_d, new_x, new_y, source, edge, ch, cl)
    density, flux_x, flux_y = new_d, new_x, new_y
    for iteration in range(ITERS):
        modes = exchange(modes)
        body = functools.partial(solve_body, slabs, places, steps, screen, iteration > 0)
        settings = dict(scratch=[pltpu.VMEM(square, f32)], n_in=7, cost=(3 * mega, 6 * nbytes), name="solve")
        shapes = [packed(3), square]
        matrices = (ch, cl, wh, wl)
        if iteration:
            modes, total = call(body, shapes, **settings)(modes, *matrices, inverse, total)
        else:
            modes, total, inverse = call(body, shapes + [square], scalars=2, **settings)(
                place, values, modes, *matrices, across, around
            )
        modes = exchange(modes)
        if iteration + 1 == ITERS:
            break
        density, flux_x, flux_y, modes, edge, kept, hat = call(
            functools.partial(middle_body, places - 1, screen), [field] * 3 + [packed(items), edge_shape, block, hat_shape],
            scratch=[pltpu.VMEM(((steps + 1) * rows + BLOCK, width), f32)] + split,
            scalars=1, n_in=14, cost=(2 * mega, 10 * nbytes), name="middle",
        )(place, modes, density, flux_x, flux_y, source, edge, kept, hat, ch, cl, *inner, scale)
    (potential,) = call(
        last_body, [field], scratch=[pltpu.VMEM((steps * rows, width), f32), pltpu.SemaphoreType.DMA((steps,))],
        n_in=8, far_out=True, cost=(mega, 3 * nbytes), name="last",
    )(modes, hat, ch, cl, *inner, scale)
    return density, flux_x, flux_y, potential


def solution(mesh):
    spec = P("tm", "space", None)
    return jax.shard_map(local, mesh=mesh, in_specs=(spec,) * 4, out_specs=(spec,) * 4, check_vma=False)
```

```python
import functools

import jax
import jax.numpy as jnp
import numpy as np
from jax import lax
from jax.experimental import pallas as pl
from jax.experimental.pallas import tpu as pltpu
from jax.sharding import PartitionSpec as P

ITERS = 3
NEWTON = 10
TAU_STEP = 1.0
SLOW_LOOP = 2.25
INTERPRET = False
GRANT = 20 << 20
KEPT = 8
TAKEN = 13
BLOCK = 16
ORDER = (1, 2, 0, 3)
BOTH = ("tm", "space")
f32 = jnp.float32
bf16 = jnp.bfloat16
NN = (((1,), (0,)), ((), ()))
NT = (((1,), (1,)), ((), ()))
TN = (((0,), (0,)), ((), ()))


def halves(value):
    high = value.astype(bf16)
    return high, (value - high.astype(f32)).astype(bf16)


def dot3(left, right, dims):
    dot = functools.partial(lax.dot_general, dimension_numbers=dims, preferred_element_type=f32)
    return dot(left[0], right[0]) + (dot(left[0], right[1]) + dot(left[1], right[0]))


def cosine_matrix(points):
    one = np.float32
    frequency = np.arange(points, dtype=one)[:, None]
    sample = np.arange(points, dtype=one)[None, :]
    scaling = np.where(frequency == 0, np.sqrt(one(1.0 / points)), np.sqrt(one(2.0 / points))).astype(one)
    angle = one(np.pi) * (sample + one(0.5)) * frequency / one(points)
    return (scaling * np.cos(angle.astype(np.float64)).astype(one)).astype(one)


def neumann_spectrum(points):
    half_angle = np.pi * np.arange(points) / (2.0 * points)
    return (4.0 * np.sin(half_angle) ** 2).astype(np.float32)


def loop_basis(length, slabs):
    rows = [np.full(length, np.sqrt(1.0 / length))]
    values = [0.0]
    moment = np.arange(length)
    for k in range(1, length // 2):
        angle = 2.0 * np.pi * ((k * moment) % length) / length
        rows += [np.sqrt(2.0 / length) * np.cos(angle), np.sqrt(2.0 / length) * np.sin(angle)]
        values += [4.0 * np.sin(np.pi * k / length) ** 2] * 2
    rows.append(np.sqrt(1.0 / length) * (-1.0) ** moment)
    values.append(4.0)
    basis = np.stack(rows).reshape(length, slabs, length // slabs).transpose(0, 2, 1).reshape(length, length)
    return basis.astype(np.float32), np.asarray(values, np.float32)


def np_halves(matrix):
    high = matrix.astype(bf16)
    return high, (matrix - high.astype(np.float32)).astype(bf16)


def call(body, outs, scratch=(), scalars=0, far=0, n_in=0, far_out=False, cost=None, **kw):
    vmem = pl.BlockSpec(memory_space=pltpu.VMEM)
    smem = pl.BlockSpec(memory_space=pltpu.SMEM)
    hbm = pl.BlockSpec(memory_space=pltpu.HBM)
    return pl.pallas_call(
        body,
        out_shape=[jax.ShapeDtypeStruct(s, f32) if far_out else pltpu.VMEM(s, f32) for s in outs],
        in_specs=[smem] * scalars + [hbm] * far + [vmem] * n_in,
        out_specs=[hbm if far_out else vmem] * len(outs),
        scratch_shapes=list(scratch),
        cost_estimate=pl.CostEstimate(flops=int(cost[0]), bytes_accessed=int(cost[1]), transcendentals=0),
        compiler_params=pltpu.CompilerParams(vmem_limit_bytes=GRANT),
        interpret=INTERPRET,
        **kw,
    )


def newton(mass, along_x, along_y):
    target = 0.5 * TAU_STEP * (along_x * along_x + along_y * along_y)
    root = jnp.maximum(mass, 0.0) + jnp.exp(jnp.log(target) * (1.0 / 3.0))
    shifted = root + TAU_STEP
    half_base = 0.5 * (mass + TAU_STEP)
    quarter = 0.25 * target
    for _ in range(NEWTON):
        half = 0.5 * shifted
        product = shifted * (shifted - half_base)
        shifted = jnp.maximum((half * product + quarter) / (product - half * half), TAU_STEP)
    root = shifted - TAU_STEP
    factor = root / shifted
    return root, factor * along_x, factor * along_y


def prox_cells(source, result, wait=None):
    steps, rows, width = result[0].shape
    chunk = 16
    per = rows // chunk

    def step(index, carry):
        t = index // per
        if wait is not None:
            pl.when(index % per == 0)(lambda: wait(t))
        span = pl.ds(pl.multiple_of((index % per) * chunk, chunk), chunk)
        out = newton(*[ref[t, span, :] for ref in source])
        for ref, value in zip(result, out):
            ref[t, span, :] = value
        return carry

    lax.fori_loop(0, steps * per, step, 0)


def send_values(y, hat_sum, qh, ql, pick, scale):
    count = y.shape[0] // 3
    lanes = y.shape[1]
    both = y[pl.ds(2, count, stride=3), :]
    outer = jnp.concatenate([y[pl.ds(0, count, stride=3), :], y[pl.ds(1, count, stride=3), :]], axis=0)
    edge = jnp.concatenate([both, pltpu.roll(both, lanes // 2, 1)], axis=0)
    sine = (qh[...], ql[...])
    high, low = (lax.dot_general(part, pick[...], NN, preferred_element_type=f32) for part in halves(edge))
    moved = high + low
    modes = dot3(halves(outer + hat_sum[...] + moved[:, lanes:]), sine, NN)
    inner = dot3(halves(modes * scale[...]), sine, NN) + moved[:, :lanes]
    return outer, inner, edge


def fill_slab(u, rows, outer, inner, edge, ch, cl):
    parts = [inner, outer] + ([] if edge is None else [edge])
    value = dot3(halves(jnp.concatenate(parts, axis=1)), (ch[...], cl[...]), TN)
    u[rows : 3 * rows, :] = value[: 2 * rows, :]
    u[:rows, :] = value[2 * rows : 3 * rows, :]
    u[3 * rows : 4 * rows, :] = value[3 * rows : 4 * rows, :]
    if edge is not None:
        u[4 * rows : 5 * rows, :] = value[4 * rows : 5 * rows, :]


def fill_plane(u, steps, rows, screen, residual_sum):
    at = (steps - 1) * rows + KEPT
    here = u[at : at + BLOCK, :]
    width = here.shape[1]
    column = lax.broadcasted_iota(jnp.int32, here.shape, 1)
    right = jnp.where(column == width - 1, here, pltpu.roll(here, width - 1, 1))
    left = jnp.where(column == 0, here, pltpu.roll(here, 1, 1))
    earlier = u[at - rows : at - rows + BLOCK, :]
    value = (here - earlier) + (here - u[at - 1 : at - 1 + BLOCK, :]) + (here - u[at + 1 : at + 1 + BLOCK, :])
    value = here + (value + (here - right) + (here - left) + screen * here - residual_sum)
    at = steps * rows + KEPT
    row = lax.broadcasted_iota(jnp.int32, here.shape, 0)
    u[at : at + BLOCK, :] = jnp.where(row < TAKEN, value, u[at : at + BLOCK, :])


def dual_step(d, fx, fy, edge, u, nd, nx, ny):
    steps, rows, width = d.shape
    below_at = (steps + 1) * rows
    above_at = below_at + steps
    end_row = lax.broadcasted_iota(jnp.int32, (rows, width), 0) == rows - 1
    end_column = lax.broadcasted_iota(jnp.int32, (rows, width), 1) == width - 1
    for t in range(steps):
        here = u[t * rows : (t + 1) * rows, :]
        later = u[(t + 1) * rows : (t + 2) * rows, :]
        below = jnp.where(end_row, u[below_at + t : below_at + t + 1, :], pltpu.roll(here, rows - 1, 0))
        right = jnp.where(end_column, here, pltpu.roll(here, width - 1, 1))
        nd[t] = d[t] - TAU_STEP * (here - later)
        nx[t] = fx[t] - TAU_STEP * (here - below)
        ny[t] = fy[t] - TAU_STEP * (here - right)
    here = u[above_at : above_at + steps, :]
    later = u[above_at + 1 : above_at + 1 + steps, :]
    below = jnp.concatenate([u[t * rows : t * rows + 1, :] for t in range(steps)], axis=0)
    right = jnp.where(end_column[:steps, :], here, pltpu.roll(here, width - 1, 1))
    return (
        edge[0] - TAU_STEP * (here - later),
        edge[1] - TAU_STEP * (here - below),
        edge[2] - TAU_STEP * (here - right),
    )


def residual_modes(place, last_place, d, fx, fy, nd, nx, ny, src, edge_x, new_edge_x, ch, cl, out, kept, hat, rh, rl):
    steps, rows, width = d.shape
    shape = (rows, width)
    row = lax.broadcasted_iota(jnp.int32, shape, 0)
    column = lax.broadcasted_iota(jnp.int32, shape, 1)
    final_row = (row == rows - 1) & (place == last_place)
    edge_bar = jnp.where(place == 0, 0.0, 2.0 * new_edge_x - edge_x)
    before = None
    for t in range(steps):
        mass = 2.0 * nd[t] - d[t]
        along_x = 2.0 * nx[t] - fx[t]
        along_y = 2.0 * ny[t] - fy[t]
        x_before = jnp.where(row == 0, edge_bar[t : t + 1, :], pltpu.roll(along_x, 1, 0))
        y_before = jnp.where(column == 0, 0.0, pltpu.roll(along_y, 1, 1))
        value = mass if before is None else mass - before
        value = value + (jnp.where(final_row, 0.0, along_x) - x_before)
        value = value + (jnp.where(column == width - 1, 0.0, along_y) - y_before)
        value = value - src[t]
        before = mass
        high, low = halves(value)
        at = ORDER.index(t) * rows
        rh[at : at + rows, :] = high
        rl[at : at + rows, :] = low
    kept[...] = value[KEPT : KEPT + BLOCK, :]
    high, low = halves(before)
    for t in (steps, steps + 1):
        rh[t * rows : (t + 1) * rows, :] = high
        rl[t * rows : (t + 1) * rows, :] = low
    modes = dot3((ch[...], cl[...]), (rh[...], rl[...]), NT)
    lanes = 2 * rows
    hat[...] = modes[:, :lanes]
    pairs = steps // 2
    count = width // 2
    group = 2 * pairs + 1
    for pair in range(pairs):
        span = slice(pair * lanes, (pair + 1) * lanes)
        out[pl.ds(pair, count, stride=group), :] = modes[:count, span]
        out[pl.ds(pairs + pair, count, stride=group), :] = modes[count:, span]
    span = slice(pairs * lanes, (pairs + 1) * lanes)
    low_half = lax.broadcasted_iota(jnp.int32, (count, lanes), 1) < rows
    out[pl.ds(2 * pairs, count, stride=group), :] = jnp.where(low_half, modes[:count, span], modes[count:, span])


def edge_body(d, fx, fy, edge):
    rows = d.shape[1]
    for k, ref in enumerate((d, fx, fy)):
        for t in range(d.shape[0]):
            edge[k, t : t + 1, :] = ref[t, rows - 1 :, :]


def stay(value):
    return value if INTERPRET else pltpu.with_memory_space_constraint(value, pltpu.HBM)


def last_rows(density, flux_x, flux_y):
    steps, rows, width = density.shape
    block = pl.BlockSpec((steps, 8, width), lambda i: (0, rows // 8 - 1, 0))
    return pl.pallas_call(
        edge_body,
        grid=(1,),
        out_shape=jax.ShapeDtypeStruct((3, steps, width), f32),
        in_specs=[block] * 3,
        out_specs=pl.BlockSpec((3, steps, width), lambda i: (0, 0, 0)),
        compiler_params=pltpu.CompilerParams(vmem_limit_bytes=GRANT),
        interpret=INTERPRET,
        name="edges",
    )(*map(stay, (density, flux_x, flux_y)))


def prox_body(
    screen, place, d, fx, fy, across, along, around, nd, nx, ny, own_d, own_x, own_y, scale, inverse, table, sems, small,
):
    steps = d.shape[0]
    width = across.shape[1]
    lanes = along.shape[1]
    length = around.shape[1]
    moves = ((d, own_d), (fx, own_x), (fy, own_y))
    tables = [
        pltpu.make_async_copy(ref, table.at[pl.ds(k, 1), pl.ds(0, ref.shape[1])], small.at[k])
        for k, ref in enumerate((across, along, around))
    ]

    def copy(k, t):
        return pltpu.make_async_copy(moves[k][0].at[t], moves[k][1].at[t], sems.at[k, t])

    for move in tables:
        move.start()
    for t in range(steps):
        for k in range(3):
            copy(k, t).start()
    for move in tables:
        move.wait()
    values = table[0:1, :]
    scale[...] = 1.0 / (jnp.broadcast_to(values, (lanes, width)).T + table[1:2, :lanes])
    turned = jnp.broadcast_to(table[2:3, :length], (width, length)).T
    lane = lax.broadcasted_iota(jnp.int32, values.shape, 1)
    for mode in range(2):
        own = jnp.sum(jnp.where(lane == place[1] + mode * (width // 2), values, 0.0), axis=1, keepdims=True)
        inverse[mode * length : (mode + 1) * length, :] = 1.0 / (turned + (values + (own + screen)))

    def wait(t):
        for k in range(3):
            copy(k, t).wait()

    prox_cells((own_d, own_x, own_y), (nd, nx, ny), wait)


def forward_body(last_place, place, d, fx, fy, nd, nx, ny, src, edge, ch, cl, out, new_edge, kept, hat, rh, rl):
    fresh = newton(edge[0], edge[1], edge[2])
    for k in range(3):
        new_edge[k] = fresh[k]
    residual_modes(place[0], last_place, d, fx, fy, nd, nx, ny, src, edge[1], fresh[1], ch, cl, out, kept, hat, rh, rl)


def middle_body(
    last_place, screen, place, y, d, fx, fy, src, edge, kept_sum, hat_sum, ch, cl, qh, ql, pick, scale,
    nd, nx, ny, out, new_edge, kept, hat, u, rh, rl,
):
    steps, rows, _ = d.shape
    fill_slab(u, rows, *send_values(y, hat_sum, qh, ql, pick, scale), ch, cl)
    at = steps * rows
    u[at + rows : at + rows + TAKEN, :] = u[at + KEPT : at + KEPT + TAKEN, :]
    fill_plane(u, steps, rows, screen, kept_sum[...])
    fresh = newton(*dual_step(d, fx, fy, edge, u, nd, nx, ny))
    for k in range(3):
        new_edge[k] = fresh[k]
    prox_cells((nd, nx, ny), (nd, nx, ny))
    residual_modes(place[0], last_place, d, fx, fy, nd, nx, ny, src, edge[1], fresh[1], ch, cl, out, kept, hat, rh, rl)
    kept[...] = kept[...] + kept_sum[...]
    hat[...] = hat[...] + hat_sum[...]


def last_body(y, hat_sum, ch, cl, qh, ql, pick, scale, u, flat, sems):
    steps, rows, _ = u.shape
    outer, inner, _ = send_values(y, hat_sum, qh, ql, pick, scale)
    fill_slab(flat, rows, outer, inner, None, ch, cl)
    copies = [pltpu.make_async_copy(flat.at[pl.ds(t * rows, rows), :], u.at[t], sems.at[t]) for t in range(steps)]
    for copy in copies:
        copy.start()
    for copy in copies:
        copy.wait()


def solve_body(slabs, places, steps, with_sum, *refs):
    if with_sum:
        z, ch, cl, wh, wl, inverse, so_far, out, total, field = refs
    else:
        z, ch, cl, wh, wl, inverse, out, total, field = refs
    length = slabs * steps
    pairs = steps // 2
    lanes = z.shape[1]
    rows = lanes // 2
    lane = lax.broadcasted_iota(jnp.int32, (slabs, lanes), 1)
    low_half = lane < rows

    def swap(a, b):
        return jnp.where(low_half, a, pltpu.roll(b, rows, 1)), jnp.where(low_half, pltpu.roll(a, rows, 1), b)

    group = 2 * pairs + 1

    def arrived(place, item):
        return z[pl.ds(place * group + item, slabs, stride=places * group), :]

    for q in range(places // 2):
        span = slice(q * lanes, (q + 1) * lanes)
        planes = swap(arrived(2 * q, 2 * pairs), arrived(2 * q + 1, 2 * pairs))
        for mode in range(2):
            for pair in range(pairs):
                item = mode * pairs + pair
                first, second = swap(arrived(2 * q, item), arrived(2 * q + 1, item))
                for t, value in zip(ORDER[2 * pair : 2 * pair + 2], (first, second)):
                    if t == 0:
                        value = value - pltpu.roll(planes[mode], 1, 0)
                    top = mode * length + t * slabs
                    field[top : top + slabs, span] = value
    cosine = (ch[...], cl[...])
    for mode in range(2):
        span = slice(mode * length, (mode + 1) * length)
        field[span, :] = dot3((wh[...], wl[...]), halves(field[span, :]), NN)
    solved = dot3(halves(field[...]), cosine, NT) * inverse[...]
    if with_sum:
        solved = solved + so_far[...]
    total[...] = solved
    field[...] = dot3(halves(solved), cosine, NN)
    for mode in range(2):
        span = slice(mode * length, (mode + 1) * length)
        field[span, :] = dot3((wh[...], wl[...]), halves(field[span, :]), TN)
    group_out = 3

    def leaving(place, item):
        return pl.ds(place * group_out + item, slabs, stride=places * group_out)

    for q in range(places // 2):
        span = slice(q * lanes, (q + 1) * lanes)
        for mode in range(2):
            at = mode * length
            end = at + (steps - 1) * slabs
            first, second = swap(field[at : at + slabs, span], field[end : end + slabs, span])
            out[leaving(2 * q, mode), :] = first
            out[leaving(2 * q + 1, mode), :] = second
        planes = swap(*[pltpu.roll(field[m * length : m * length + slabs, span], slabs - 1, 0) for m in range(2)])
        for spot, value in zip((2 * q, 2 * q + 1), planes):
            after = (spot + 1) * rows if spot + 1 < places else (spot + 1) * rows - 1
            before = max(spot * rows - 1, 0)
            for mode in range(2):
                top = mode * length
                at = mode * rows + KEPT
                for t in range(steps):
                    column = field[top + t * slabs : top + (t + 1) * slabs, after : after + 1]
                    value = jnp.where(lane == at + t, column, value)
                for t in range(steps + 1):
                    column = field[top + (t % steps) * slabs : top + (t % steps + 1) * slabs, before : before + 1]
                    if t == steps:
                        column = pltpu.roll(jnp.broadcast_to(column, (slabs, lanes)), slabs - 1, 0)
                    value = jnp.where(lane == at + steps + t, column, value)
                for k, (t, line) in enumerate(((1, 0), (1, rows - 1), (2, 0), (2, rows - 1))):
                    line = spot * rows + line
                    column = field[top + t * slabs : top + (t + 1) * slabs, line : line + 1]
                    value = jnp.where(lane == at + 2 * steps + 1 + k, column, value)
            out[leaving(spot, 2), :] = value


def local(density, flux_x, flux_y, source):
    steps, rows, width = density.shape
    slabs = lax.axis_size("tm")
    places = lax.axis_size("space")
    length = steps * slabs
    screen = SLOW_LOOP / float(length * length)
    order = np.concatenate([np.arange(0, width, 2), np.arange(1, width, 2)])
    ch, cl = (jnp.asarray(m) for m in np_halves(cosine_matrix(width)[order]))
    basis, loop_values = loop_basis(length, slabs)
    wh, wl = (jnp.asarray(m) for m in np_halves(basis))
    spectrum = neumann_spectrum(width)
    place = lax.axis_index("space")
    first = lax.axis_index("tm") * places + place
    count = np.arange(rows)
    gaps = rows - 1
    sine = np.sqrt(2.0 / gaps) * np.sin(np.pi * (np.outer(count, count) % (2 * gaps)) / gaps)
    sine[0] = sine[-1] = sine[:, 0] = sine[:, -1] = 0.0
    lines = np.sqrt(0.5) * np.block([[sine, sine], [sine, -sine]])
    lanes_of = 2 * rows
    pick = np.zeros((lanes_of, 2 * lanes_of), np.float32)
    for spot, place_of, line in ((0, 0, 1), (1, rows - 1, rows - 2), (2, rows, rows + 1), (3, 2 * rows - 1, 2 * rows - 2)):
        pick[KEPT + 2 * steps + 1 + spot, (place_of, lanes_of + line)] = 1.0
    inner = [jnp.asarray(m) for m in np_halves(lines.astype(np.float32))]
    inner.append(jnp.asarray(pick.astype(bf16)))
    stiffness = 2.0 - 2.0 * np.cos(np.pi * count / gaps)
    along = jnp.asarray((np.concatenate([1.0 + stiffness, 3.0 + stiffness]) + screen).astype(np.float32)[None, :])
    across = jnp.asarray(spectrum[order][None, :])
    around = jnp.asarray(loop_values[None, :])
    place = jnp.stack([place, first]).astype(jnp.int32)
    nbytes = density.size * 4
    mega = density.size * width * 6
    field = (steps, rows, width)
    edge_shape = (3, steps, width)
    lanes = 2 * rows
    devices = slabs * places

    def packed(items):
        return (devices * items, lanes)

    items = steps + 1

    def exchange(value):
        shape = value.shape
        value = value.reshape(devices, 1, shape[0] // devices * lanes)
        value = lax.all_to_all(value, BOTH, split_axis=0, concat_axis=0, tiled=True)
        return value.reshape(shape)

    edge = lax.ppermute(last_rows(density, flux_x, flux_y), "space", [(i, i + 1) for i in range(places - 1)])
    split = [pltpu.VMEM(((steps + 2) * rows, width), bf16)] * 2
    block = (BLOCK, width)
    square = (2 * length, width)
    hat_shape = (width, lanes)
    new_d, new_x, new_y, density, flux_x, flux_y, scale, inverse = call(
        functools.partial(prox_body, screen), [field] * 6 + [hat_shape, square],
        scratch=[pltpu.VMEM((8, width), f32), pltpu.SemaphoreType.DMA((3, steps)), pltpu.SemaphoreType.DMA((3,))],
        scalars=1, far=6, cost=(density.size * 200, 6 * nbytes), name="prox",
    )(place, *map(stay, (density, flux_x, flux_y, across, along, around)))
    modes, edge, kept, hat = call(
        functools.partial(forward_body, places - 1), [packed(items), edge_shape, block, hat_shape],
        scratch=split, scalars=1, n_in=10, cost=(mega, 8 * nbytes), name="forward",
    )(place, density, flux_x, flux_y, new_d, new_x, new_y, source, edge, ch, cl)
    density, flux_x, flux_y = new_d, new_x, new_y
    for iteration in range(ITERS):
        modes = exchange(modes)
        carried = (total,) if iteration else ()
        modes, total = call(
            functools.partial(solve_body, slabs, places, steps, iteration > 0), [packed(3), square],
            scratch=[pltpu.VMEM(square, f32)], n_in=6 + len(carried), cost=(3 * mega, 6 * nbytes), name="solve",
        )(modes, ch, cl, wh, wl, inverse, *carried)
        modes = exchange(modes)
        if iteration + 1 == ITERS:
            break
        density, flux_x, flux_y, modes, edge, kept, hat = call(
            functools.partial(middle_body, places - 1, screen), [field] * 3 + [packed(items), edge_shape, block, hat_shape],
            scratch=[pltpu.VMEM(((steps + 1) * rows + BLOCK, width), f32)] + split,
            scalars=1, n_in=14, cost=(2 * mega, 10 * nbytes), name="middle",
        )(place, modes, density, flux_x, flux_y, source, edge, kept, hat, ch, cl, *inner, scale)
    (potential,) = call(
        last_body, [field], scratch=[pltpu.VMEM((steps * rows, width), f32), pltpu.SemaphoreType.DMA((steps,))],
        n_in=8, far_out=True, cost=(mega, 3 * nbytes), name="last",
    )(modes, hat, ch, cl, *inner, scale)
    return density, flux_x, flux_y, potential


def solution(mesh):
    spec = P("tm", "space", None)
    return jax.shard_map(local, mesh=mesh, in_specs=(spec,) * 4, out_specs=(spec,) * 4, check_vma=False)
```

```python
import functools

import jax
import jax.numpy as jnp
import numpy as np
from jax import lax
from jax.experimental import pallas as pl
from jax.experimental.pallas import tpu as pltpu
from jax.sharding import PartitionSpec as P

ITERS = 3
NEWTON = 10
TAU_STEP = 1.0
SLOW_LOOP = 2.25
INTERPRET = False
GRANT = 20 << 20
KEPT = 8
TAKEN = 13
BLOCK = 16
ORDER = (1, 2, 0, 3)
BOTH = ("tm", "space")
f32 = jnp.float32
bf16 = jnp.bfloat16
NN = (((1,), (0,)), ((), ()))
NT = (((1,), (1,)), ((), ()))
TN = (((0,), (0,)), ((), ()))


def halves(value):
    high = value.astype(bf16)
    return high, (value - high.astype(f32)).astype(bf16)


def dot3(left, right, dims):
    dot = functools.partial(lax.dot_general, dimension_numbers=dims, preferred_element_type=f32)
    return dot(left[0], right[0]) + (dot(left[0], right[1]) + dot(left[1], right[0]))


def cosine_matrix(points):
    one = np.float32
    frequency = np.arange(points, dtype=one)[:, None]
    sample = np.arange(points, dtype=one)[None, :]
    scaling = np.where(frequency == 0, np.sqrt(one(1.0 / points)), np.sqrt(one(2.0 / points))).astype(one)
    angle = one(np.pi) * (sample + one(0.5)) * frequency / one(points)
    return (scaling * np.cos(angle.astype(np.float64)).astype(one)).astype(one)


def neumann_spectrum(points):
    half_angle = np.pi * np.arange(points) / (2.0 * points)
    return (4.0 * np.sin(half_angle) ** 2).astype(np.float32)


def loop_basis(length, slabs):
    rows = [np.full(length, np.sqrt(1.0 / length))]
    values = [0.0]
    moment = np.arange(length)
    for k in range(1, length // 2):
        angle = 2.0 * np.pi * ((k * moment) % length) / length
        rows += [np.sqrt(2.0 / length) * np.cos(angle), np.sqrt(2.0 / length) * np.sin(angle)]
        values += [4.0 * np.sin(np.pi * k / length) ** 2] * 2
    rows.append(np.sqrt(1.0 / length) * (-1.0) ** moment)
    values.append(4.0)
    basis = np.stack(rows).reshape(length, slabs, length // slabs).transpose(0, 2, 1).reshape(length, length)
    return basis.astype(np.float32), np.asarray(values, np.float32)


def np_halves(matrix):
    high = matrix.astype(bf16)
    return high, (matrix - high.astype(np.float32)).astype(bf16)


def call(body, outs, scratch=(), scalars=0, far=0, n_in=0, far_out=0, cost=None, **kw):
    vmem = pl.BlockSpec(memory_space=pltpu.VMEM)
    smem = pl.BlockSpec(memory_space=pltpu.SMEM)
    hbm = pl.BlockSpec(memory_space=pltpu.HBM)
    return pl.pallas_call(
        body,
        out_shape=[jax.ShapeDtypeStruct(s, f32) if k < far_out else pltpu.VMEM(s, f32) for k, s in enumerate(outs)],
        in_specs=[smem] * scalars + [hbm] * far + [vmem] * n_in,
        out_specs=[hbm] * far_out + [vmem] * (len(outs) - far_out),
        scratch_shapes=list(scratch),
        cost_estimate=pl.CostEstimate(flops=int(cost[0]), bytes_accessed=int(cost[1]), transcendentals=0),
        compiler_params=pltpu.CompilerParams(vmem_limit_bytes=GRANT),
        interpret=INTERPRET,
        **kw,
    )


def newton(mass, along_x, along_y):
    target = 0.5 * TAU_STEP * (along_x * along_x + along_y * along_y)
    root = jnp.maximum(mass, 0.0) + jnp.exp(jnp.log(target) * (1.0 / 3.0))
    shifted = root + TAU_STEP
    half_base = 0.5 * (mass + TAU_STEP)
    quarter = 0.25 * target
    for _ in range(NEWTON):
        half = 0.5 * shifted
        product = shifted * (shifted - half_base)
        shifted = jnp.maximum((half * product + quarter) / (product - half * half), TAU_STEP)
    root = shifted - TAU_STEP
    factor = root / shifted
    return root, factor * along_x, factor * along_y


def prox_cells(source, result, wait=None, ready=None):
    steps, rows, width = result[0].shape
    chunk = 16
    per = rows // chunk

    def step(index, carry):
        t = index // per
        if wait is not None:
            pl.when(index % per == 0)(lambda: wait(t))
        span = pl.ds(pl.multiple_of((index % per) * chunk, chunk), chunk)
        out = newton(*[ref[t, span, :] for ref in source])
        for ref, value in zip(result, out):
            ref[t, span, :] = value
        if ready is not None:
            pl.when(index % per == per - 1)(lambda: ready(t))
        return carry

    lax.fori_loop(0, steps * per, step, 0)


def send_values(y, hat_sum, qh, ql, pick, scale):
    count = y.shape[0] // 3
    lanes = y.shape[1]
    both = y[pl.ds(2, count, stride=3), :]
    outer = jnp.concatenate([y[pl.ds(0, count, stride=3), :], y[pl.ds(1, count, stride=3), :]], axis=0)
    edge = jnp.concatenate([both, pltpu.roll(both, lanes // 2, 1)], axis=0)
    sine = (qh[...], ql[...])
    high, low = (lax.dot_general(part, pick[...], NN, preferred_element_type=f32) for part in halves(edge))
    moved = high + low
    modes = dot3(halves(outer + hat_sum[...] + moved[:, lanes:]), sine, NN)
    inner = dot3(halves(modes * scale[...]), sine, NN) + moved[:, :lanes]
    return outer, inner, edge


def fill_slab(u, rows, outer, inner, edge, ch, cl, ready=lambda *steps: None):
    cosine = (ch[...], cl[...])
    value = dot3(halves(outer), cosine, TN)
    u[:rows, :] = value[:rows, :]
    u[3 * rows : 4 * rows, :] = value[rows:, :]
    ready(0, 3)
    u[rows : 3 * rows, :] = dot3(halves(inner), cosine, TN)
    ready(1, 2)
    if edge is not None:
        u[4 * rows : 5 * rows, :] = dot3(halves(edge), cosine, TN)[:rows, :]


def fill_plane(u, steps, rows, screen, residual_sum):
    at = (steps - 1) * rows + KEPT
    here = u[at : at + BLOCK, :]
    width = here.shape[1]
    column = lax.broadcasted_iota(jnp.int32, here.shape, 1)
    right = jnp.where(column == width - 1, here, pltpu.roll(here, width - 1, 1))
    left = jnp.where(column == 0, here, pltpu.roll(here, 1, 1))
    earlier = u[at - rows : at - rows + BLOCK, :]
    value = (here - earlier) + (here - u[at - 1 : at - 1 + BLOCK, :]) + (here - u[at + 1 : at + 1 + BLOCK, :])
    value = here + (value + (here - right) + (here - left) + screen * here - residual_sum)
    at = steps * rows + KEPT
    row = lax.broadcasted_iota(jnp.int32, here.shape, 0)
    u[at : at + BLOCK, :] = jnp.where(row < TAKEN, value, u[at : at + BLOCK, :])


def dual_step(d, fx, fy, edge, u, nd, nx, ny):
    steps, rows, width = d.shape
    below_at = (steps + 1) * rows
    above_at = below_at + steps
    end_row = lax.broadcasted_iota(jnp.int32, (rows, width), 0) == rows - 1
    end_column = lax.broadcasted_iota(jnp.int32, (rows, width), 1) == width - 1
    for t in range(steps):
        here = u[t * rows : (t + 1) * rows, :]
        later = u[(t + 1) * rows : (t + 2) * rows, :]
        below = jnp.where(end_row, u[below_at + t : below_at + t + 1, :], pltpu.roll(here, rows - 1, 0))
        right = jnp.where(end_column, here, pltpu.roll(here, width - 1, 1))
        nd[t] = d[t] - TAU_STEP * (here - later)
        nx[t] = fx[t] - TAU_STEP * (here - below)
        ny[t] = fy[t] - TAU_STEP * (here - right)
    here = u[above_at : above_at + steps, :]
    later = u[above_at + 1 : above_at + 1 + steps, :]
    below = jnp.concatenate([u[t * rows : t * rows + 1, :] for t in range(steps)], axis=0)
    right = jnp.where(end_column[:steps, :], here, pltpu.roll(here, width - 1, 1))
    return (
        edge[0] - TAU_STEP * (here - later),
        edge[1] - TAU_STEP * (here - below),
        edge[2] - TAU_STEP * (here - right),
    )


def residual_modes(place, last_place, d, fx, fy, nd, nx, ny, src, edge_x, new_edge_x, ch, cl, out, kept, hat, rh, rl):
    steps, rows, width = d.shape
    shape = (rows, width)
    row = lax.broadcasted_iota(jnp.int32, shape, 0)
    column = lax.broadcasted_iota(jnp.int32, shape, 1)
    final_row = (row == rows - 1) & (place == last_place)
    edge_bar = jnp.where(place == 0, 0.0, 2.0 * new_edge_x - edge_x)
    before = None
    for t in range(steps):
        mass = 2.0 * nd[t] - d[t]
        along_x = 2.0 * nx[t] - fx[t]
        along_y = 2.0 * ny[t] - fy[t]
        x_before = jnp.where(row == 0, edge_bar[t : t + 1, :], pltpu.roll(along_x, 1, 0))
        y_before = jnp.where(column == 0, 0.0, pltpu.roll(along_y, 1, 1))
        value = mass if before is None else mass - before
        value = value + (jnp.where(final_row, 0.0, along_x) - x_before)
        value = value + (jnp.where(column == width - 1, 0.0, along_y) - y_before)
        value = value - src[t]
        before = mass
        high, low = halves(value)
        at = ORDER.index(t) * rows
        rh[at : at + rows, :] = high
        rl[at : at + rows, :] = low
    kept[...] = value[KEPT : KEPT + BLOCK, :]
    high, low = halves(before)
    for t in (steps, steps + 1):
        rh[t * rows : (t + 1) * rows, :] = high
        rl[t * rows : (t + 1) * rows, :] = low
    modes = dot3((ch[...], cl[...]), (rh[...], rl[...]), NT)
    lanes = 2 * rows
    hat[...] = modes[:, :lanes]
    pairs = steps // 2
    count = width // 2
    group = 2 * pairs + 1
    for pair in range(pairs):
        span = slice(pair * lanes, (pair + 1) * lanes)
        out[pl.ds(pair, count, stride=group), :] = modes[:count, span]
        out[pl.ds(pairs + pair, count, stride=group), :] = modes[count:, span]
    span = slice(pairs * lanes, (pairs + 1) * lanes)
    low_half = lax.broadcasted_iota(jnp.int32, (count, lanes), 1) < rows
    out[pl.ds(2 * pairs, count, stride=group), :] = jnp.where(low_half, modes[:count, span], modes[count:, span])


def edge_body(d, fx, fy, edge):
    rows = d.shape[1]
    for k, ref in enumerate((d, fx, fy)):
        for t in range(d.shape[0]):
            edge[k, t : t + 1, :] = ref[t, rows - 1 :, :]


def stay(value):
    return value if INTERPRET else pltpu.with_memory_space_constraint(value, pltpu.HBM)


def last_rows(density, flux_x, flux_y):
    steps, rows, width = density.shape
    block = pl.BlockSpec((steps, 8, width), lambda i: (0, rows // 8 - 1, 0))
    return pl.pallas_call(
        edge_body,
        grid=(1,),
        out_shape=jax.ShapeDtypeStruct((3, steps, width), f32),
        in_specs=[block] * 3,
        out_specs=pl.BlockSpec((3, steps, width), lambda i: (0, 0, 0)),
        compiler_params=pltpu.CompilerParams(vmem_limit_bytes=GRANT),
        interpret=INTERPRET,
        name="edges",
    )(*map(stay, (density, flux_x, flux_y)))


def prox_body(
    screen, place, d, fx, fy, across, along, around, nd, nx, ny, own_d, own_x, own_y, scale, inverse, table, sems, small,
):
    steps = d.shape[0]
    width = across.shape[1]
    lanes = along.shape[1]
    length = around.shape[1]
    moves = ((d, own_d), (fx, own_x), (fy, own_y))
    tables = [
        pltpu.make_async_copy(ref, table.at[pl.ds(k, 1), pl.ds(0, ref.shape[1])], small.at[k])
        for k, ref in enumerate((across, along, around))
    ]

    def copy(k, t):
        return pltpu.make_async_copy(moves[k][0].at[t], moves[k][1].at[t], sems.at[k, t])

    for move in tables:
        move.start()
    for t in range(steps):
        for k in range(3):
            copy(k, t).start()
    for move in tables:
        move.wait()
    values = table[0:1, :]
    scale[...] = 1.0 / (jnp.broadcast_to(values, (lanes, width)).T + table[1:2, :lanes])
    turned = jnp.broadcast_to(table[2:3, :length], (width, length)).T
    lane = lax.broadcasted_iota(jnp.int32, values.shape, 1)
    for mode in range(2):
        own = jnp.sum(jnp.where(lane == place[1] + mode * (width // 2), values, 0.0), axis=1, keepdims=True)
        inverse[mode * length : (mode + 1) * length, :] = 1.0 / (turned + (values + (own + screen)))

    def wait(t):
        for k in range(3):
            copy(k, t).wait()

    prox_cells((own_d, own_x, own_y), (nd, nx, ny), wait)


def forward_body(last_place, place, d, fx, fy, nd, nx, ny, src, edge, ch, cl, out, new_edge, kept, hat, rh, rl):
    fresh = newton(edge[0], edge[1], edge[2])
    for k in range(3):
        new_edge[k] = fresh[k]
    residual_modes(place[0], last_place, d, fx, fy, nd, nx, ny, src, edge[1], fresh[1], ch, cl, out, kept, hat, rh, rl)


def middle_body(
    last_place, screen, place, y, d, fx, fy, src, edge, kept_sum, hat_sum, ch, cl, qh, ql, pick, scale,
    out_d, out_x, out_y, out, new_edge, kept, hat, u, rh, rl, *leave,
):
    nd, nx, ny = leave[:3] if leave else (out_d, out_x, out_y)
    steps, rows, _ = d.shape
    fill_slab(u, rows, *send_values(y, hat_sum, qh, ql, pick, scale), ch, cl)
    at = steps * rows
    u[at + rows : at + rows + TAKEN, :] = u[at + KEPT : at + KEPT + TAKEN, :]
    fill_plane(u, steps, rows, screen, kept_sum[...])
    fresh = newton(*dual_step(d, fx, fy, edge, u, nd, nx, ny))
    for k in range(3):
        new_edge[k] = fresh[k]

    def move(k, t):
        return pltpu.make_async_copy((nd, nx, ny)[k].at[t], (out_d, out_x, out_y)[k].at[t], leave[3].at[k, t])

    def ready(t):
        for k in range(3):
            move(k, t).start()

    prox_cells((nd, nx, ny), (nd, nx, ny), ready=ready if leave else None)
    residual_modes(place[0], last_place, d, fx, fy, nd, nx, ny, src, edge[1], fresh[1], ch, cl, out, kept, hat, rh, rl)
    kept[...] = kept[...] + kept_sum[...]
    hat[...] = hat[...] + hat_sum[...]
    if leave:
        for t in range(steps):
            for k in range(3):
                move(k, t).wait()


def last_body(y, hat_sum, ch, cl, qh, ql, pick, scale, u, flat, sems):
    steps, rows, _ = u.shape
    outer, inner, _ = send_values(y, hat_sum, qh, ql, pick, scale)

    def move(t):
        return pltpu.make_async_copy(flat.at[pl.ds(t * rows, rows), :], u.at[t], sems.at[t])

    def ready(*which):
        for t in which:
            move(t).start()

    fill_slab(flat, rows, outer, inner, None, ch, cl, ready)
    for t in range(steps):
        move(t).wait()


def solve_body(slabs, places, steps, with_sum, *refs):
    if with_sum:
        z, ch, cl, wh, wl, inverse, so_far, out, total, field = refs
    else:
        z, ch, cl, wh, wl, inverse, out, total, field = refs
    length = slabs * steps
    pairs = steps // 2
    lanes = z.shape[1]
    rows = lanes // 2
    lane = lax.broadcasted_iota(jnp.int32, (slabs, lanes), 1)
    low_half = lane < rows

    def swap(a, b):
        return jnp.where(low_half, a, pltpu.roll(b, rows, 1)), jnp.where(low_half, pltpu.roll(a, rows, 1), b)

    group = 2 * pairs + 1

    def arrived(place, item):
        return z[pl.ds(place * group + item, slabs, stride=places * group), :]

    for q in range(places // 2):
        span = slice(q * lanes, (q + 1) * lanes)
        planes = swap(arrived(2 * q, 2 * pairs), arrived(2 * q + 1, 2 * pairs))
        for mode in range(2):
            for pair in range(pairs):
                item = mode * pairs + pair
                first, second = swap(arrived(2 * q, item), arrived(2 * q + 1, item))
                for t, value in zip(ORDER[2 * pair : 2 * pair + 2], (first, second)):
                    if t == 0:
                        value = value - pltpu.roll(planes[mode], 1, 0)
                    top = mode * length + t * slabs
                    field[top : top + slabs, span] = value
    cosine = (ch[...], cl[...])
    for mode in range(2):
        span = slice(mode * length, (mode + 1) * length)
        field[span, :] = dot3((wh[...], wl[...]), halves(field[span, :]), NN)
    solved = dot3(halves(field[...]), cosine, NT) * inverse[...]
    if with_sum:
        solved = solved + so_far[...]
    total[...] = solved
    field[...] = dot3(halves(solved), cosine, NN)
    for mode in range(2):
        span = slice(mode * length, (mode + 1) * length)
        field[span, :] = dot3((wh[...], wl[...]), halves(field[span, :]), TN)
    group_out = 3

    def leaving(place, item):
        return pl.ds(place * group_out + item, slabs, stride=places * group_out)

    for q in range(places // 2):
        span = slice(q * lanes, (q + 1) * lanes)
        for mode in range(2):
            at = mode * length
            end = at + (steps - 1) * slabs
            first, second = swap(field[at : at + slabs, span], field[end : end + slabs, span])
            out[leaving(2 * q, mode), :] = first
            out[leaving(2 * q + 1, mode), :] = second
        planes = swap(*[pltpu.roll(field[m * length : m * length + slabs, span], slabs - 1, 0) for m in range(2)])
        for spot, value in zip((2 * q, 2 * q + 1), planes):
            after = (spot + 1) * rows if spot + 1 < places else (spot + 1) * rows - 1
            before = max(spot * rows - 1, 0)
            for mode in range(2):
                top = mode * length
                at = mode * rows + KEPT
                for t in range(steps):
                    column = field[top + t * slabs : top + (t + 1) * slabs, after : after + 1]
                    value = jnp.where(lane == at + t, column, value)
                for t in range(steps + 1):
                    column = field[top + (t % steps) * slabs : top + (t % steps + 1) * slabs, before : before + 1]
                    if t == steps:
                        column = pltpu.roll(jnp.broadcast_to(column, (slabs, lanes)), slabs - 1, 0)
                    value = jnp.where(lane == at + steps + t, column, value)
                for k, (t, line) in enumerate(((1, 0), (1, rows - 1), (2, 0), (2, rows - 1))):
                    line = spot * rows + line
                    column = field[top + t * slabs : top + (t + 1) * slabs, line : line + 1]
                    value = jnp.where(lane == at + 2 * steps + 1 + k, column, value)
            out[leaving(spot, 2), :] = value


def local(density, flux_x, flux_y, source):
    steps, rows, width = density.shape
    slabs = lax.axis_size("tm")
    places = lax.axis_size("space")
    length = steps * slabs
    screen = SLOW_LOOP / float(length * length)
    order = np.concatenate([np.arange(0, width, 2), np.arange(1, width, 2)])
    ch, cl = (jnp.asarray(m) for m in np_halves(cosine_matrix(width)[order]))
    basis, loop_values = loop_basis(length, slabs)
    wh, wl = (jnp.asarray(m) for m in np_halves(basis))
    spectrum = neumann_spectrum(width)
    place = lax.axis_index("space")
    first = lax.axis_index("tm") * places + place
    count = np.arange(rows)
    gaps = rows - 1
    sine = np.sqrt(2.0 / gaps) * np.sin(np.pi * (np.outer(count, count) % (2 * gaps)) / gaps)
    sine[0] = sine[-1] = sine[:, 0] = sine[:, -1] = 0.0
    lines = np.sqrt(0.5) * np.block([[sine, sine], [sine, -sine]])
    lanes_of = 2 * rows
    pick = np.zeros((lanes_of, 2 * lanes_of), np.float32)
    for spot, place_of, line in ((0, 0, 1), (1, rows - 1, rows - 2), (2, rows, rows + 1), (3, 2 * rows - 1, 2 * rows - 2)):
        pick[KEPT + 2 * steps + 1 + spot, (place_of, lanes_of + line)] = 1.0
    inner = [jnp.asarray(m) for m in np_halves(lines.astype(np.float32))]
    inner.append(jnp.asarray(pick.astype(bf16)))
    stiffness = 2.0 - 2.0 * np.cos(np.pi * count / gaps)
    along = jnp.asarray((np.concatenate([1.0 + stiffness, 3.0 + stiffness]) + screen).astype(np.float32)[None, :])
    across = jnp.asarray(spectrum[order][None, :])
    around = jnp.asarray(loop_values[None, :])
    place = jnp.stack([place, first]).astype(jnp.int32)
    nbytes = density.size * 4
    mega = density.size * width * 6
    field = (steps, rows, width)
    edge_shape = (3, steps, width)
    lanes = 2 * rows
    devices = slabs * places

    def packed(items):
        return (devices * items, lanes)

    items = steps + 1

    def exchange(value):
        shape = value.shape
        value = value.reshape(devices, 1, shape[0] // devices * lanes)
        value = lax.all_to_all(value, BOTH, split_axis=0, concat_axis=0, tiled=True)
        return value.reshape(shape)

    edge = lax.ppermute(last_rows(density, flux_x, flux_y), "space", [(i, i + 1) for i in range(places - 1)])
    split = [pltpu.VMEM(((steps + 2) * rows, width), bf16)] * 2
    block = (BLOCK, width)
    square = (2 * length, width)
    hat_shape = (width, lanes)
    new_d, new_x, new_y, density, flux_x, flux_y, scale, inverse = call(
        functools.partial(prox_body, screen), [field] * 6 + [hat_shape, square],
        scratch=[pltpu.VMEM((8, width), f32), pltpu.SemaphoreType.DMA((3, steps)), pltpu.SemaphoreType.DMA((3,))],
        scalars=1, far=6, cost=(density.size * 200, 6 * nbytes), name="prox",
    )(place, *map(stay, (density, flux_x, flux_y, across, along, around)))
    modes, edge, kept, hat = call(
        functools.partial(forward_body, places - 1), [packed(items), edge_shape, block, hat_shape],
        scratch=split, scalars=1, n_in=10, cost=(mega, 8 * nbytes), name="forward",
    )(place, density, flux_x, flux_y, new_d, new_x, new_y, source, edge, ch, cl)
    density, flux_x, flux_y = new_d, new_x, new_y
    for iteration in range(ITERS):
        modes = exchange(modes)
        carried = (total,) if iteration else ()
        modes, total = call(
            functools.partial(solve_body, slabs, places, steps, iteration > 0), [packed(3), square],
            scratch=[pltpu.VMEM(square, f32)], n_in=6 + len(carried), cost=(3 * mega, 6 * nbytes), name="solve",
        )(modes, ch, cl, wh, wl, inverse, *carried)
        modes = exchange(modes)
        if iteration + 1 == ITERS:
            break
        leave = []
        if iteration + 2 == ITERS:
            leave = [pltpu.VMEM(field, f32)] * 3 + [pltpu.SemaphoreType.DMA((3, steps))]
        density, flux_x, flux_y, modes, edge, kept, hat = call(
            functools.partial(middle_body, places - 1, screen), [field] * 3 + [packed(items), edge_shape, block, hat_shape],
            scratch=[pltpu.VMEM(((steps + 1) * rows + BLOCK, width), f32)] + split + leave,
            scalars=1, n_in=14, far_out=3 if leave else 0, cost=(2 * mega, 10 * nbytes), name="middle",
        )(place, modes, density, flux_x, flux_y, source, edge, kept, hat, ch, cl, *inner, scale)
    (potential,) = call(
        last_body, [field], scratch=[pltpu.VMEM((steps * rows, width), f32), pltpu.SemaphoreType.DMA((steps,))],
        n_in=8, far_out=1, cost=(mega, 3 * nbytes), name="last",
    )(modes, hat, ch, cl, *inner, scale)
    return density, flux_x, flux_y, potential


def solution(mesh):
    spec = P("tm", "space", None)
    return jax.shard_map(local, mesh=mesh, in_specs=(spec,) * 4, out_specs=(spec,) * 4, check_vma=False)
```

```python
import functools

import jax
import jax.numpy as jnp
import numpy as np
from jax import lax
from jax.experimental import pallas as pl
from jax.experimental.pallas import tpu as pltpu
from jax.sharding import PartitionSpec as P

ITERS = 3
NEWTON = 10
TAU_STEP = 1.0
SLOW_LOOP = 2.25
INTERPRET = False
GRANT = 20 << 20
KEPT = 8
TAKEN = 13
BLOCK = 16
ORDER = (1, 2, 0, 3)
BOTH = ("tm", "space")
f32 = jnp.float32
bf16 = jnp.bfloat16
NN = (((1,), (0,)), ((), ()))
NT = (((1,), (1,)), ((), ()))
TN = (((0,), (0,)), ((), ()))


def halves(value):
    high = value.astype(bf16)
    return high, (value - high.astype(f32)).astype(bf16)


def dot3(left, right, dims):
    dot = functools.partial(lax.dot_general, dimension_numbers=dims, preferred_element_type=f32)
    return dot(left[0], right[0]) + (dot(left[0], right[1]) + dot(left[1], right[0]))


def cosine_matrix(points):
    one = np.float32
    frequency = np.arange(points, dtype=one)[:, None]
    sample = np.arange(points, dtype=one)[None, :]
    scaling = np.where(frequency == 0, np.sqrt(one(1.0 / points)), np.sqrt(one(2.0 / points))).astype(one)
    angle = one(np.pi) * (sample + one(0.5)) * frequency / one(points)
    return (scaling * np.cos(angle.astype(np.float64)).astype(one)).astype(one)


def neumann_spectrum(points):
    half_angle = np.pi * np.arange(points) / (2.0 * points)
    return (4.0 * np.sin(half_angle) ** 2).astype(np.float32)


def loop_basis(length, slabs):
    rows = [np.full(length, np.sqrt(1.0 / length))]
    values = [0.0]
    moment = np.arange(length)
    for k in range(1, length // 2):
        angle = 2.0 * np.pi * ((k * moment) % length) / length
        rows += [np.sqrt(2.0 / length) * np.cos(angle), np.sqrt(2.0 / length) * np.sin(angle)]
        values += [4.0 * np.sin(np.pi * k / length) ** 2] * 2
    rows.append(np.sqrt(1.0 / length) * (-1.0) ** moment)
    values.append(4.0)
    basis = np.stack(rows).reshape(length, slabs, length // slabs).transpose(0, 2, 1).reshape(length, length)
    return basis.astype(np.float32), np.asarray(values, np.float32)


def np_halves(matrix):
    high = matrix.astype(bf16)
    return high, (matrix - high.astype(np.float32)).astype(bf16)


def call(body, outs, scratch=(), scalars=0, far=0, n_in=0, far_out=0, cost=None, **kw):
    vmem = pl.BlockSpec(memory_space=pltpu.VMEM)
    smem = pl.BlockSpec(memory_space=pltpu.SMEM)
    hbm = pl.BlockSpec(memory_space=pltpu.HBM)
    return pl.pallas_call(
        body,
        out_shape=[jax.ShapeDtypeStruct(s, f32) if k < far_out else pltpu.VMEM(s, f32) for k, s in enumerate(outs)],
        in_specs=[smem] * scalars + [hbm] * far + [vmem] * n_in,
        out_specs=[hbm] * far_out + [vmem] * (len(outs) - far_out),
        scratch_shapes=list(scratch),
        cost_estimate=pl.CostEstimate(flops=int(cost[0]), bytes_accessed=int(cost[1]), transcendentals=0),
        compiler_params=pltpu.CompilerParams(vmem_limit_bytes=GRANT),
        interpret=INTERPRET,
        **kw,
    )


def newton(mass, along_x, along_y):
    target = 0.5 * TAU_STEP * (along_x * along_x + along_y * along_y)
    root = jnp.maximum(mass, 0.0) + jnp.exp(jnp.log(target) * (1.0 / 3.0))
    shifted = root + TAU_STEP
    half_base = 0.5 * (mass + TAU_STEP)
    quarter = 0.25 * target
    for _ in range(NEWTON):
        half = 0.5 * shifted
        product = shifted * (shifted - half_base)
        shifted = jnp.maximum((half * product + quarter) / (product - half * half), TAU_STEP)
    root = shifted - TAU_STEP
    factor = root / shifted
    return root, factor * along_x, factor * along_y


def prox_cells(source, result, wait=None, ready=None):
    steps, rows, width = result[0].shape
    chunk = 16
    per = rows // chunk

    def step(index, carry):
        t = index // per
        if wait is not None:
            pl.when(index % per == 0)(lambda: wait(t))
        span = pl.ds(pl.multiple_of((index % per) * chunk, chunk), chunk)
        out = newton(*[ref[t, span, :] for ref in source])
        for ref, value in zip(result, out):
            ref[t, span, :] = value
        if ready is not None:
            pl.when(index % per == per - 1)(lambda: ready(t))
        return carry

    lax.fori_loop(0, steps * per, step, 0)


def send_values(y, hat_sum, qh, ql, pick, scale):
    count = y.shape[0] // 3
    lanes = y.shape[1]
    both = y[pl.ds(2, count, stride=3), :]
    outer = jnp.concatenate([y[pl.ds(0, count, stride=3), :], y[pl.ds(1, count, stride=3), :]], axis=0)
    edge = jnp.concatenate([both, pltpu.roll(both, lanes // 2, 1)], axis=0)
    sine = (qh[...], ql[...])
    high, low = (lax.dot_general(part, pick[...], NN, preferred_element_type=f32) for part in halves(edge))
    moved = high + low
    modes = dot3(halves(outer + hat_sum[...] + moved[:, lanes:]), sine, NN)
    inner = dot3(halves(modes * scale[...]), sine, NN) + moved[:, :lanes]
    return outer, inner, edge


def fill_slab(u, rows, outer, inner, edge, ch, cl, ready=lambda *steps: None):
    cosine = (ch[...], cl[...])
    value = dot3(halves(outer), cosine, TN)
    u[:rows, :] = value[:rows, :]
    u[3 * rows : 4 * rows, :] = value[rows:, :]
    ready(0, 3)
    u[rows : 3 * rows, :] = dot3(halves(inner), cosine, TN)
    ready(1, 2)
    if edge is not None:
        u[4 * rows : 5 * rows, :] = dot3(halves(edge), cosine, TN)[:rows, :]


def fill_plane(u, steps, rows, screen, residual_sum):
    at = (steps - 1) * rows + KEPT
    here = u[at : at + BLOCK, :]
    width = here.shape[1]
    column = lax.broadcasted_iota(jnp.int32, here.shape, 1)
    right = jnp.where(column == width - 1, here, pltpu.roll(here, width - 1, 1))
    left = jnp.where(column == 0, here, pltpu.roll(here, 1, 1))
    earlier = u[at - rows : at - rows + BLOCK, :]
    value = (here - earlier) + (here - u[at - 1 : at - 1 + BLOCK, :]) + (here - u[at + 1 : at + 1 + BLOCK, :])
    value = here + (value + (here - right) + (here - left) + screen * here - residual_sum)
    at = steps * rows + KEPT
    row = lax.broadcasted_iota(jnp.int32, here.shape, 0)
    u[at : at + BLOCK, :] = jnp.where(row < TAKEN, value, u[at : at + BLOCK, :])


def dual_step(d, fx, fy, edge, u, nd, nx, ny):
    steps, rows, width = d.shape
    below_at = (steps + 1) * rows
    above_at = below_at + steps
    end_row = lax.broadcasted_iota(jnp.int32, (rows, width), 0) == rows - 1
    end_column = lax.broadcasted_iota(jnp.int32, (rows, width), 1) == width - 1
    for t in range(steps):
        here = u[t * rows : (t + 1) * rows, :]
        later = u[(t + 1) * rows : (t + 2) * rows, :]
        below = jnp.where(end_row, u[below_at + t : below_at + t + 1, :], pltpu.roll(here, rows - 1, 0))
        right = jnp.where(end_column, here, pltpu.roll(here, width - 1, 1))
        nd[t] = d[t] - TAU_STEP * (here - later)
        nx[t] = fx[t] - TAU_STEP * (here - below)
        ny[t] = fy[t] - TAU_STEP * (here - right)
    here = u[above_at : above_at + steps, :]
    later = u[above_at + 1 : above_at + 1 + steps, :]
    below = jnp.concatenate([u[t * rows : t * rows + 1, :] for t in range(steps)], axis=0)
    right = jnp.where(end_column[:steps, :], here, pltpu.roll(here, width - 1, 1))
    return (
        edge[0] - TAU_STEP * (here - later),
        edge[1] - TAU_STEP * (here - below),
        edge[2] - TAU_STEP * (here - right),
    )


def residual_modes(place, last_place, d, fx, fy, nd, nx, ny, src, edge_x, new_edge_x, ch, cl, out, kept, hat, rh, rl):
    steps, rows, width = d.shape
    shape = (rows, width)
    row = lax.broadcasted_iota(jnp.int32, shape, 0)
    column = lax.broadcasted_iota(jnp.int32, shape, 1)
    final_row = (row == rows - 1) & (place == last_place)
    edge_bar = jnp.where(place == 0, 0.0, 2.0 * new_edge_x - edge_x)
    before = None
    for t in range(steps):
        mass = 2.0 * nd[t] - d[t]
        along_x = 2.0 * nx[t] - fx[t]
        along_y = 2.0 * ny[t] - fy[t]
        x_before = jnp.where(row == 0, edge_bar[t : t + 1, :], pltpu.roll(along_x, 1, 0))
        y_before = jnp.where(column == 0, 0.0, pltpu.roll(along_y, 1, 1))
        value = mass if before is None else mass - before
        value = value + (jnp.where(final_row, 0.0, along_x) - x_before)
        value = value + (jnp.where(column == width - 1, 0.0, along_y) - y_before)
        value = value - src[t]
        before = mass
        high, low = halves(value)
        at = ORDER.index(t) * rows
        rh[at : at + rows, :] = high
        rl[at : at + rows, :] = low
    kept[...] = value[KEPT : KEPT + BLOCK, :]
    high, low = halves(before)
    for t in (steps, steps + 1):
        rh[t * rows : (t + 1) * rows, :] = high
        rl[t * rows : (t + 1) * rows, :] = low
    modes = dot3((ch[...], cl[...]), (rh[...], rl[...]), NT)
    lanes = 2 * rows
    hat[...] = modes[:, :lanes]
    pairs = steps // 2
    count = width // 2
    group = 2 * pairs + 1
    for pair in range(pairs):
        span = slice(pair * lanes, (pair + 1) * lanes)
        out[pl.ds(pair, count, stride=group), :] = modes[:count, span]
        out[pl.ds(pairs + pair, count, stride=group), :] = modes[count:, span]
    span = slice(pairs * lanes, (pairs + 1) * lanes)
    low_half = lax.broadcasted_iota(jnp.int32, (count, lanes), 1) < rows
    out[pl.ds(2 * pairs, count, stride=group), :] = jnp.where(low_half, modes[:count, span], modes[count:, span])


def edge_body(d, fx, fy, edge):
    rows = d.shape[1]
    for k, ref in enumerate((d, fx, fy)):
        for t in range(d.shape[0]):
            edge[k, t : t + 1, :] = ref[t, rows - 1 :, :]


def stay(value):
    return value if INTERPRET else pltpu.with_memory_space_constraint(value, pltpu.HBM)


def last_rows(density, flux_x, flux_y):
    steps, rows, width = density.shape
    block = pl.BlockSpec((steps, 8, width), lambda i: (0, rows // 8 - 1, 0))
    return pl.pallas_call(
        edge_body,
        grid=(1,),
        out_shape=jax.ShapeDtypeStruct((3, steps, width), f32),
        in_specs=[block] * 3,
        out_specs=pl.BlockSpec((3, steps, width), lambda i: (0, 0, 0)),
        compiler_params=pltpu.CompilerParams(vmem_limit_bytes=GRANT),
        interpret=INTERPRET,
        name="edges",
    )(*map(stay, (density, flux_x, flux_y)))


def prox_body(
    screen, place, d, fx, fy, across, along, around, nd, nx, ny, own_d, own_x, own_y, scale, inverse, table, sems, small,
):
    steps = d.shape[0]
    width = across.shape[1]
    lanes = along.shape[1]
    length = around.shape[1]
    moves = ((d, own_d), (fx, own_x), (fy, own_y))
    tables = [
        pltpu.make_async_copy(ref, table.at[pl.ds(k, 1), pl.ds(0, ref.shape[1])], small.at[k])
        for k, ref in enumerate((across, along, around))
    ]

    def copy(k, t):
        return pltpu.make_async_copy(moves[k][0].at[t], moves[k][1].at[t], sems.at[k, t])

    for move in tables:
        move.start()
    for t in range(steps):
        for k in range(3):
            copy(k, t).start()
    for move in tables:
        move.wait()
    values = table[0:1, :]
    scale[...] = 1.0 / (jnp.broadcast_to(values, (lanes, width)).T + table[1:2, :lanes])
    turned = jnp.broadcast_to(table[2:3, :length], (width, length)).T
    lane = lax.broadcasted_iota(jnp.int32, values.shape, 1)
    for mode in range(2):
        own = jnp.sum(jnp.where(lane == place[1] + mode * (width // 2), values, 0.0), axis=1, keepdims=True)
        inverse[mode * length : (mode + 1) * length, :] = 1.0 / (turned + (values + (own + screen)))

    def wait(t):
        for k in range(3):
            copy(k, t).wait()

    prox_cells((own_d, own_x, own_y), (nd, nx, ny), wait)


def forward_body(last_place, place, d, fx, fy, nd, nx, ny, src, edge, ch, cl, out, new_edge, kept, hat, rh, rl):
    fresh = newton(edge[0], edge[1], edge[2])
    for k in range(3):
        new_edge[k] = fresh[k]
    residual_modes(place[0], last_place, d, fx, fy, nd, nx, ny, src, edge[1], fresh[1], ch, cl, out, kept, hat, rh, rl)


def middle_body(
    last_place, screen, place, y, d, fx, fy, src, edge, kept_sum, hat_sum, ch, cl, qh, ql, pick, scale,
    out_d, out_x, out_y, out, new_edge, kept, hat, u, rh, rl, *leave,
):
    nd, nx, ny = leave[:3] if leave else (out_d, out_x, out_y)
    steps, rows, _ = d.shape
    fill_slab(u, rows, *send_values(y, hat_sum, qh, ql, pick, scale), ch, cl)
    at = steps * rows
    u[at + rows : at + rows + TAKEN, :] = u[at + KEPT : at + KEPT + TAKEN, :]
    fill_plane(u, steps, rows, screen, kept_sum[...])
    fresh = newton(*dual_step(d, fx, fy, edge, u, nd, nx, ny))
    for k in range(3):
        new_edge[k] = fresh[k]

    def move(k, t):
        return pltpu.make_async_copy((nd, nx, ny)[k].at[t], (out_d, out_x, out_y)[k].at[t], leave[3].at[k, t])

    def ready(t):
        for k in range(3):
            move(k, t).start()

    prox_cells((nd, nx, ny), (nd, nx, ny), ready=ready if leave else None)
    residual_modes(place[0], last_place, d, fx, fy, nd, nx, ny, src, edge[1], fresh[1], ch, cl, out, kept, hat, rh, rl)
    kept[...] = kept[...] + kept_sum[...]
    hat[...] = hat[...] + hat_sum[...]
    if leave:
        for t in range(steps):
            for k in range(3):
                move(k, t).wait()


def last_body(y, hat_sum, ch, cl, qh, ql, pick, scale, u, flat, sems):
    steps, rows, _ = u.shape
    outer, inner, _ = send_values(y, hat_sum, qh, ql, pick, scale)

    def move(t):
        return pltpu.make_async_copy(flat.at[pl.ds(t * rows, rows), :], u.at[t], sems.at[t])

    def ready(*which):
        for t in which:
            move(t).start()

    fill_slab(flat, rows, outer, inner, None, ch, cl, ready)
    for t in range(steps):
        move(t).wait()


def solve_body(slabs, places, steps, with_sum, *refs):
    if with_sum:
        z, ch, cl, wh, wl, inverse, so_far, out, total, field = refs
    else:
        z, ch, cl, wh, wl, inverse, out, total, field = refs
    length = slabs * steps
    pairs = steps // 2
    lanes = z.shape[1]
    rows = lanes // 2
    lane = lax.broadcasted_iota(jnp.int32, (slabs, lanes), 1)
    low_half = lane < rows

    def swap(a, b):
        return jnp.where(low_half, a, pltpu.roll(b, rows, 1)), jnp.where(low_half, pltpu.roll(a, rows, 1), b)

    group = 2 * pairs + 1

    def arrived(place, item):
        return z[pl.ds(place * group + item, slabs, stride=places * group), :]

    for q in range(places // 2):
        span = slice(q * lanes, (q + 1) * lanes)
        planes = swap(arrived(2 * q, 2 * pairs), arrived(2 * q + 1, 2 * pairs))
        for mode in range(2):
            for pair in range(pairs):
                item = mode * pairs + pair
                first, second = swap(arrived(2 * q, item), arrived(2 * q + 1, item))
                for t, value in zip(ORDER[2 * pair : 2 * pair + 2], (first, second)):
                    if t == 0:
                        value = value - pltpu.roll(planes[mode], 1, 0)
                    top = mode * length + t * slabs
                    field[top : top + slabs, span] = value
    cosine = (ch[...], cl[...])
    for mode in range(2):
        span = slice(mode * length, (mode + 1) * length)
        field[span, :] = dot3((wh[...], wl[...]), halves(field[span, :]), NN)
    solved = dot3(halves(field[...]), cosine, NT) * inverse[...]
    if with_sum:
        solved = solved + so_far[...]
    total[...] = solved
    field[...] = dot3(halves(solved), cosine, NN)
    for mode in range(2):
        span = slice(mode * length, (mode + 1) * length)
        field[span, :] = dot3((wh[...], wl[...]), halves(field[span, :]), TN)
    group_out = 3

    def leaving(place, item):
        return pl.ds(place * group_out + item, slabs, stride=places * group_out)

    for q in range(places // 2):
        span = slice(q * lanes, (q + 1) * lanes)
        for mode in range(2):
            at = mode * length
            end = at + (steps - 1) * slabs
            first, second = swap(field[at : at + slabs, span], field[end : end + slabs, span])
            out[leaving(2 * q, mode), :] = first
            out[leaving(2 * q + 1, mode), :] = second
        planes = swap(*[pltpu.roll(field[m * length : m * length + slabs, span], slabs - 1, 0) for m in range(2)])
        for spot, value in zip((2 * q, 2 * q + 1), planes):
            after = (spot + 1) * rows if spot + 1 < places else (spot + 1) * rows - 1
            before = max(spot * rows - 1, 0)
            for mode in range(2):
                top = mode * length
                at = mode * rows + KEPT
                for t in range(steps):
                    column = field[top + t * slabs : top + (t + 1) * slabs, after : after + 1]
                    value = jnp.where(lane == at + t, column, value)
                for t in range(steps + 1):
                    column = field[top + (t % steps) * slabs : top + (t % steps + 1) * slabs, before : before + 1]
                    if t == steps:
                        column = pltpu.roll(jnp.broadcast_to(column, (slabs, lanes)), slabs - 1, 0)
                    value = jnp.where(lane == at + steps + t, column, value)
                for k, (t, line) in enumerate(((1, 0), (1, rows - 1), (2, 0), (2, rows - 1))):
                    line = spot * rows + line
                    column = field[top + t * slabs : top + (t + 1) * slabs, line : line + 1]
                    value = jnp.where(lane == at + 2 * steps + 1 + k, column, value)
            out[leaving(spot, 2), :] = value


def local(density, flux_x, flux_y, source):
    steps, rows, width = density.shape
    slabs = lax.axis_size("tm")
    places = lax.axis_size("space")
    length = steps * slabs
    screen = SLOW_LOOP / float(length * length)
    order = np.concatenate([np.arange(0, width, 2), np.arange(1, width, 2)])
    ch, cl = (jnp.asarray(m) for m in np_halves(cosine_matrix(width)[order]))
    basis, loop_values = loop_basis(length, slabs)
    wh, wl = (jnp.asarray(m) for m in np_halves(basis))
    spectrum = neumann_spectrum(width)
    place = lax.axis_index("space")
    first = lax.axis_index("tm") * places + place
    count = np.arange(rows)
    gaps = rows - 1
    sine = np.sqrt(2.0 / gaps) * np.sin(np.pi * (np.outer(count, count) % (2 * gaps)) / gaps)
    sine[0] = sine[-1] = sine[:, 0] = sine[:, -1] = 0.0
    lines = np.sqrt(0.5) * np.block([[sine, sine], [sine, -sine]])
    lanes_of = 2 * rows
    pick = np.zeros((lanes_of, 2 * lanes_of), np.float32)
    for spot, place_of, line in ((0, 0, 1), (1, rows - 1, rows - 2), (2, rows, rows + 1), (3, 2 * rows - 1, 2 * rows - 2)):
        pick[KEPT + 2 * steps + 1 + spot, (place_of, lanes_of + line)] = 1.0
    inner = [jnp.asarray(m) for m in np_halves(lines.astype(np.float32))]
    inner.append(jnp.asarray(pick.astype(bf16)))
    stiffness = 2.0 - 2.0 * np.cos(np.pi * count / gaps)
    along = jnp.asarray((np.concatenate([1.0 + stiffness, 3.0 + stiffness]) + screen).astype(np.float32)[None, :])
    across = jnp.asarray(spectrum[order][None, :])
    around = jnp.asarray(loop_values[None, :])
    place = jnp.stack([place, first]).astype(jnp.int32)
    nbytes = density.size * 4
    mega = density.size * width * 6
    field = (steps, rows, width)
    edge_shape = (3, steps, width)
    lanes = 2 * rows
    devices = slabs * places

    def packed(items):
        return (devices * items, lanes)

    items = steps + 1

    def exchange(value):
        shape = value.shape
        value = value.reshape(devices, 1, shape[0] // devices * lanes)
        value = lax.all_to_all(value, BOTH, split_axis=0, concat_axis=0, tiled=True)
        return value.reshape(shape)

    edge = lax.ppermute(last_rows(density, flux_x, flux_y), "space", [(i, i + 1) for i in range(places - 1)])
    split = [pltpu.VMEM(((steps + 2) * rows, width), bf16)] * 2
    block = (BLOCK, width)
    square = (2 * length, width)
    hat_shape = (width, lanes)
    new_d, new_x, new_y, density, flux_x, flux_y, scale, inverse = call(
        functools.partial(prox_body, screen), [field] * 6 + [hat_shape, square],
        scratch=[pltpu.VMEM((8, width), f32), pltpu.SemaphoreType.DMA((3, steps)), pltpu.SemaphoreType.DMA((3,))],
        scalars=1, far=6, cost=(density.size * 200, 6 * nbytes), name="prox",
    )(place, *map(stay, (density, flux_x, flux_y, across, along, around)))
    modes, edge, kept, hat = call(
        functools.partial(forward_body, places - 1), [packed(items), edge_shape, block, hat_shape],
        scratch=split, scalars=1, n_in=10, cost=(mega, 8 * nbytes), name="forward",
    )(place, density, flux_x, flux_y, new_d, new_x, new_y, source, edge, ch, cl)
    density, flux_x, flux_y = new_d, new_x, new_y
    for iteration in range(ITERS):
        modes = exchange(modes)
        carried = (total,) if iteration else ()
        kept_total = [square] if iteration + 1 < ITERS else []
        modes, *rest = call(
            functools.partial(solve_body, slabs, places, steps, iteration > 0), [packed(3)] + kept_total,
            scratch=[pltpu.VMEM(square, f32)] * (3 - len(kept_total) - 1), n_in=6 + len(carried), cost=(3 * mega, 6 * nbytes), name="solve",
        )(modes, ch, cl, wh, wl, inverse, *carried)
        total = rest[0] if rest else None
        modes = exchange(modes)
        if iteration + 1 == ITERS:
            break
        leave = []
        if iteration + 2 == ITERS:
            leave = [pltpu.VMEM(field, f32)] * 3 + [pltpu.SemaphoreType.DMA((3, steps))]
        density, flux_x, flux_y, modes, edge, kept, hat = call(
            functools.partial(middle_body, places - 1, screen), [field] * 3 + [packed(items), edge_shape, block, hat_shape],
            scratch=[pltpu.VMEM(((steps + 1) * rows + BLOCK, width), f32)] + split + leave,
            scalars=1, n_in=14, far_out=3 if leave else 0, cost=(2 * mega, 10 * nbytes), name="middle",
        )(place, modes, density, flux_x, flux_y, source, edge, kept, hat, ch, cl, *inner, scale)
    (potential,) = call(
        last_body, [field], scratch=[pltpu.VMEM((steps * rows, width), f32), pltpu.SemaphoreType.DMA((steps,))],
        n_in=8, far_out=1, cost=(mega, 3 * nbytes), name="last",
    )(modes, hat, ch, cl, *inner, scale)
    return density, flux_x, flux_y, potential


def solution(mesh):
    spec = P("tm", "space", None)
    return jax.shard_map(local, mesh=mesh, in_specs=(spec,) * 4, out_specs=(spec,) * 4, check_vma=False)
```
